512 devices in a mesh: grp: 64 (over y, z), tp: 8 (over x, core).
Axes of the slice: x: 4, y: 8, z: 8, core: 2. Of those that a mesh axis runs over, the one named last changes fastest.
Arguments:
- normed_token_input: bfloat16 [65536, 4096], P('grp', 'tp'), may hold values from -6 to 6
- queries: bfloat16 [65536, 4096], P('grp', 'tp'), may hold values from -6 to 6
- fresh_token_keys: bfloat16 [65536, 1024], P('grp', 'tp'), may hold values from -6 to 6
- fresh_token_values: bfloat16 [65536, 1024], P('grp', 'tp'), may hold values from -6 to 6
- token_request_index: int32 [65536], P('grp'), may hold values from 0 to 255, never falling along the last dimension, each value on 1 to 1024 neighbouring positions
- prefix_page_cache: bfloat16 [128, 2, 128, 1024], P('grp', None, None, 'tp'), may hold values from -6 to 6
- adapter_down_weight: bfloat16 [128, 16, 4096], P('grp', None, 'tp'), may hold values from -0.09375 to 0.09375
- adapter_up_weight: bfloat16 [128, 16, 4096], P('grp', None, 'tp'), may hold values from -1.5 to 1.5
- group_page_list: int32 [64, 4], replicated, may hold values from 0 to 127, as said below
- group_adapter_list: int32 [64, 4], replicated, may hold values from 0 to 127, as said below
- page_entry_index: int32 [256], replicated, may hold values from 0 to 3
- adapter_entry_index: int32 [256], replicated, may hold values from 0 to 3
Outputs:
- attended: bfloat16 [65536, 4096], P('grp', 'tp')
The draws below stay inside these ranges and needn't reach their ends.
Inputs may be any that keep to these rules, and one draw needn't show every extreme that they name: `group_page_list`: the 4 pages of a row lie with distinct owners: page // 2 differs within a row. `group_adapter_list`: the 4 adapters of a row lie with distinct owners: adapter // 2 differs within a row.
All inputs are finite; a program needn't handle non-finite values.
Results may differ from the reference program's by a relative error of at most 0.0065.
Values may be sent and summed in bfloat16 or wider, within the bound.
A program may use at most 64 MiB of HBM per device.

```python
import math
import jax
import jax.numpy as jnp
import numpy as np
from jax import lax

MODEL_WIDTH = 4096
QUERY_HEADS = 32
KV_HEADS = 8
HEAD_WIDTH = 128
ADAPTER_RANK = 16
PAGE = 128
PG_USE = 4
ADAPTERS_LISTED = 4
SLOTS_DEV = 2
TOK_G = 1024
GROUPS = 64
TOKENS = 65536
POOL = 128
ADAPTER_TOTAL = 128
REQS = 256
QUERY_WIDTH = 4096
KVW = 1024


def build_table(key, salt, columns):
    folded = jax.random.fold_in(key, salt)
    first_key, second_key = jax.random.split(folded)
    starting = jax.random.randint(first_key, (GROUPS,), 0, GROUPS)
    starting = starting.at[0].set(GROUPS - 1)
    owners = (starting[:, None] + jnp.arange(columns, dtype=jnp.int32)[None, :]) % GROUPS
    within = jax.random.randint(second_key, (GROUPS, columns), 0, SLOTS_DEV)
    within = within.at[0, 0].set(SLOTS_DEV - 1).at[0, 1].set(0)
    return (owners * SLOTS_DEV + within).astype(jnp.int32)


def draw_group_page_list(key, part):
    return build_table(key, 11, PG_USE)


def draw_group_adapter_list(key, part):
    return build_table(key, 23, ADAPTERS_LISTED)


def draw_queries(key, part):
    base_key = jax.random.fold_in(key, 5)
    values = jnp.clip(jax.random.normal(base_key, (TOKENS, QUERY_HEADS * HEAD_WIDTH), jnp.float32), -6.0, 6.0)
    return values.astype(jnp.bfloat16)


def draw_prefix_page_cache(key, part):
    base_key = jax.random.fold_in(key, 9)
    array_shape = (POOL, 2, PAGE, KV_HEADS * HEAD_WIDTH)
    values = jnp.clip(jax.random.normal(base_key, array_shape, jnp.float32), -6.0, 6.0)
    return values.astype(jnp.bfloat16)


def touch_ends(entries, stream_key, smallest, top_value):
    index_at = [jax.random.randint(jax.random.fold_in(stream_key, axis), (), 0, length) for axis, length in enumerate(entries.shape)]
    widest = entries.shape.index(max(entries.shape))
    neighbour = index_at[:widest] + [(index_at[widest] + 1) % entries.shape[widest]] + index_at[widest + 1:]
    return entries.at[tuple(index_at)].set(smallest).at[tuple(neighbour)].set(top_value)


def block_scale(own_key, extent, cuts, least, largest):
    level = 1.0
    for dim, parts in cuts:
        draws = jax.random.uniform(jax.random.fold_in(jax.random.fold_in(own_key, 6), dim), (parts,), jnp.float32, least / len(cuts), largest / len(cuts))
        level = level * jnp.repeat(jnp.exp(draws), extent[dim] // parts).reshape((-1,) + (1,) * (len(extent) - 1 - dim))
    return level


def length_profile(number_of, total, limit, skew):
    portions = [(1 << 20) // math.isqrt(standing ** skew) + 1 for standing in range(2, number_of + 1)]
    spare, counts = total - limit - (number_of - 1), [1] * (number_of - 1)
    while spare > 0:
        free = [i for i in range(number_of - 1) if counts[i] < limit]
        whole, left = sum([portions[i] for i in free]), spare
        for i in free:
            more = min(limit - counts[i], max(1, left * portions[i] // whole), spare)
            counts[i] = counts[i] + more
            spare = spare - more
    return np.array([limit] + counts)


def uneven_parts(stream_key, count, total, limit, slope):
    if count == 2:
        one = jax.random.randint(stream_key, (), max(1, total - limit), min(limit, total - 1) + 1)
        return jnp.stack([one, total - one])
    lengths = jnp.asarray(length_profile(count, total, limit, slope), jnp.int32)
    couples = (count - 1) // 2
    source_of, taker = lengths[1:1 + 2 * couples:2], lengths[2:2 + 2 * couples:2]
    slack = jnp.minimum(source_of - 1, limit - taker)
    moved = jax.random.randint(jax.random.fold_in(stream_key, 1), (couples,), 0, 1 << 20) % (slack + 1)
    lengths = lengths.at[1:1 + 2 * couples:2].set(source_of - moved).at[2:2 + 2 * couples:2].set(taker + moved)
    return lengths[jax.random.permutation(jax.random.fold_in(stream_key, 2), count)]


def bell_draw(key, dims, deviation, limit, cuts=(), held_as=jnp.bfloat16):
    array = jax.random.normal(key, dims, jnp.float32) * deviation
    if len(cuts) > 0:
        array = block_scale(key, dims, cuts, -0.22, 0.18) * array
    return jnp.clip(array, min=-limit, max=limit).astype(held_as)


def setup_inputs(seed: int = 0) -> dict:
    splits = jax.random.split(jax.random.key(seed), 13)
    return {
        "normed_token_input": bell_draw(splits[0], (TOKENS, MODEL_WIDTH), 1.0, 6.0, ((0, 64), (1, 8))),
        "queries": draw_queries(jax.random.fold_in(splits[12], 71), 0),
        "fresh_token_keys": bell_draw(splits[2], (TOKENS, KVW), 1.0, 6.0, ((0, 64), (1, 8))),
        "fresh_token_values": bell_draw(splits[3], (TOKENS, KVW), 1.0, 6.0, ((0, 64), (1, 8))),
        "token_request_index": jnp.searchsorted(jnp.cumsum(uneven_parts(splits[4], REQS, TOKENS, TOK_G, 1)), jnp.arange(TOKENS), side="right").astype(jnp.int32),
        "prefix_page_cache": draw_prefix_page_cache(jax.random.fold_in(splits[12], 71), 0),
        "adapter_down_weight": bell_draw(splits[6], (ADAPTER_TOTAL, ADAPTER_RANK, MODEL_WIDTH), MODEL_WIDTH ** -0.5, 0.09375, ((0, 64), (2, 8))),
        "adapter_up_weight": bell_draw(splits[7], (ADAPTER_TOTAL, ADAPTER_RANK, QUERY_WIDTH), ADAPTER_RANK ** -0.5, 1.5, ((0, 64), (2, 8))),
        "group_page_list": draw_group_page_list(jax.random.fold_in(splits[12], 71), 0),
        "group_adapter_list": draw_group_adapter_list(jax.random.fold_in(splits[12], 71), 0),
        "page_entry_index": touch_ends(jax.random.randint(splits[10], (REQS,), 0, PG_USE), jax.random.fold_in(splits[10], 1), 0, PG_USE - 1).astype(jnp.int32),
        "adapter_entry_index": touch_ends(jax.random.randint(splits[11], (REQS,), 0, ADAPTERS_LISTED), jax.random.fold_in(splits[11], 1), 0, ADAPTERS_LISTED - 1).astype(jnp.int32),
    }


adapter_scale = 0.5


def group_attention(query_rows, keys_all, values_all, visible):
    tokens = query_rows.shape[0]
    per_kv = QUERY_HEADS // KV_HEADS
    stacked = query_rows.reshape(tokens, QUERY_HEADS, HEAD_WIDTH).transpose(1, 0, 2)

    def one_head(position):
        query_head = lax.dynamic_index_in_dim(stacked, position, 0, keepdims=False)
        key_head = lax.dynamic_index_in_dim(keys_all, position // per_kv, 0, keepdims=False)
        value_head = lax.dynamic_index_in_dim(values_all, position // per_kv, 0, keepdims=False)
        scores = jnp.einsum("qd,kd->qk", query_head, key_head, preferred_element_type=jnp.float32)
        scores = jnp.where(visible, scores * (HEAD_WIDTH ** -0.5), jnp.float32(-1e30))
        highest = jnp.max(scores, axis=1, keepdims=True)
        expo = jnp.where(visible, jnp.exp(scores - highest), jnp.float32(0.0))
        weights = (expo / jnp.sum(expo, axis=1, keepdims=True)).astype(jnp.bfloat16)
        return jnp.dot(weights, value_head, preferred_element_type=jnp.float32).astype(jnp.bfloat16)

    result = lax.map(one_head, jnp.arange(QUERY_HEADS, dtype=jnp.int32))
    return result.transpose(1, 0, 2).reshape(tokens, QUERY_HEADS * HEAD_WIDTH)


def reference(normed_token_input, queries, fresh_token_keys, fresh_token_values, token_request_index, prefix_page_cache, adapter_down_weight, adapter_up_weight, group_page_list, group_adapter_list, page_entry_index, adapter_entry_index):
    groups = GROUPS
    kvw = KV_HEADS * HEAD_WIDTH
    hidden_g = normed_token_input.reshape(groups, TOK_G, MODEL_WIDTH)
    query_g = queries.reshape(groups, TOK_G, QUERY_HEADS * HEAD_WIDTH)
    keys_g = fresh_token_keys.reshape(groups, TOK_G, kvw)
    values_g = fresh_token_values.reshape(groups, TOK_G, kvw)
    segs_g = token_request_index.reshape(groups, TOK_G)
    keys_prev = jnp.concatenate([jnp.zeros_like(keys_g[:1]), keys_g[:-1]], 0)
    values_prev = jnp.concatenate([jnp.zeros_like(values_g[:1]), values_g[:-1]], 0)
    segs_prev = jnp.concatenate([jnp.zeros_like(segs_g[:1]), segs_g[:-1] + 1], 0)

    def one_group(inputs):
        hidden, query_base, keys, values, segs, prev_keys, prev_values, prev_segs, page_row, adapter_entry_row = inputs
        pages = prefix_page_cache[page_row]
        down_factors = adapter_down_weight[adapter_entry_row].reshape(ADAPTERS_LISTED * ADAPTER_RANK, MODEL_WIDTH)
        up_factors = adapter_up_weight[adapter_entry_row].reshape(ADAPTERS_LISTED * ADAPTER_RANK, QUERY_HEADS * HEAD_WIDTH)
        page_of = page_entry_index[segs]
        adapter_of = adapter_entry_index[segs]
        adapter_mask = (adapter_of[:, None] == jnp.arange(ADAPTERS_LISTED, dtype=jnp.int32)[None, :]).astype(jnp.float32)
        expanded = jnp.repeat(adapter_mask, ADAPTER_RANK, axis=1)
        lowrank = (jnp.dot(hidden, down_factors.T, preferred_element_type=jnp.float32) * expanded).astype(jnp.bfloat16)
        query_update = jnp.dot(lowrank, up_factors, preferred_element_type=jnp.float32)
        query_adapted = (query_base.astype(jnp.float32) + adapter_scale * query_update).astype(jnp.bfloat16)
        page_keys = pages[:, 0].reshape(PG_USE * PAGE, kvw)
        page_values = pages[:, 1].reshape(PG_USE * PAGE, kvw)
        keys_all = jnp.concatenate([page_keys, prev_keys, keys], 0).reshape(-1, KV_HEADS, HEAD_WIDTH).transpose(1, 0, 2)
        values_all = jnp.concatenate([page_values, prev_values, values], 0).reshape(-1, KV_HEADS, HEAD_WIDTH).transpose(1, 0, 2)
        page_cols = jnp.arange(PG_USE * PAGE, dtype=jnp.int32) // PAGE
        see_page = page_of[:, None] == page_cols[None, :]
        see_prev = prev_segs[None, :] == segs[:, None] + 1
        order = jnp.arange(TOK_G, dtype=jnp.int32)
        see_own = (segs[None, :] == segs[:, None]) & (order[None, :] <= order[:, None])
        visible = jnp.concatenate([see_page, see_prev, see_own], 1)
        return group_attention(query_adapted, keys_all, values_all, visible)

    result = lax.map(one_group, (hidden_g, query_g, keys_g, values_g, segs_g, keys_prev, values_prev, segs_prev, group_page_list, group_adapter_list))
    return result.reshape(TOKENS, QUERY_HEADS * HEAD_WIDTH)
```

```python
import functools
import math

import jax
import jax.numpy as jnp
from jax import lax
from jax.experimental import pallas as pl
from jax.experimental.pallas import tpu as pltpu
from jax.sharding import PartitionSpec as P

PER_KV = 4
HEAD_WIDTH = 128
PAGE = 128
BLOCK = 128
ADAPTER_SCALE = 0.5
MESH = pl.DeviceIdType.MESH
F32 = jnp.float32
BF16 = jnp.bfloat16


def ring_split(n, heavy_right):
    more, fewer = n // 2, (n - 1) // 2
    return (more, fewer) if heavy_right else (fewer, more)


def token_codes(ids_row, table_columns):
    requests = table_columns.shape[0]
    numbers = lax.broadcasted_iota(jnp.int32, (requests, ids_row.shape[1]), 0)
    return jnp.sum(jnp.where(numbers == ids_row, table_columns, 0), axis=0, keepdims=True)


def as_columns(row):
    return jnp.broadcast_to(row, (128, row.shape[1])).T


class Gather:
    def __init__(self, table, pos, n, right_id, left_id, split, send, recv):
        self.rights, self.lefts = split
        self.copies = []
        for s in range(1, max(split) + 1):
            now = []
            for way, (count, peer) in enumerate(((self.rights, right_id), (self.lefts, left_id))):
                if s <= count:
                    origin = lax.rem(pos - (s - 1) + n, n) if way == 0 else lax.rem(pos + (s - 1), n)
                    at = s - 1 if way == 0 else self.rights + s - 1
                    now.append(
                        pltpu.make_async_remote_copy(
                            src_ref=table.at[origin],
                            dst_ref=table.at[origin],
                            send_sem=send.at[at],
                            recv_sem=recv.at[at],
                            device_id=peer,
                            device_id_type=MESH,
                        )
                    )
                else:
                    now.append(None)
            self.copies.append(now)
        self.steps = len(self.copies)

    def start(self, s):
        for copy in self.copies[s]:
            if copy is not None:
                copy.start()

    def forward(self, s):
        for way, copy in enumerate(self.copies[s]):
            if copy is not None:
                copy.wait_recv()
                if s + 1 < self.steps and self.copies[s + 1][way] is not None:
                    self.copies[s + 1][way].start()

    def finish(self):
        for now in self.copies:
            for copy in now:
                if copy is not None:
                    copy.wait_send()


class Slots:
    def __init__(self, table, lists, slots, pos, n, right_id, left_id, split, send, recv, group_at, index_of, place_of):
        self.table, self.lists, self.slots, self.pos, self.n = table, lists, slots, pos, n
        self.split = split
        self.group_at, self.index_of, self.place_of = group_at, index_of, place_of
        self.copies = []
        for way, (count, peer) in enumerate(((split[0], right_id), (split[1], left_id))):
            base = 0 if way == 0 else split[0] + 1
            sems = 0 if way == 0 else split[0]
            self.copies.append(
                [
                    pltpu.make_async_remote_copy(
                        src_ref=slots.at[base + s],
                        dst_ref=slots.at[base + s + 1],
                        send_sem=send.at[sems + s],
                        recv_sem=recv.at[sems + s],
                        device_id=peer,
                        device_id_type=MESH,
                    )
                    for s in range(count)
                ]
            )
        self.steps = max(split)

    def fill(self, way, s):
        count = self.split[way]
        base = 0 if way == 0 else self.split[0] + 1
        away = count - s
        target = lax.rem(self.pos + away, self.n) if way == 0 else lax.rem(self.pos - away + self.n, self.n)
        group = self.group_at(target)
        for k in range(self.lists.shape[1]):
            item = self.lists[group, k]
            mine = self.table[self.index_of(item)]
            if s > 0:
                mine = jnp.where(self.place_of(item) == self.pos, mine, self.slots[base + s, k])
            self.slots[base + s, k] = mine

    def start(self):
        for way in (0, 1):
            if self.split[way] > 0:
                self.fill(way, 0)
                self.copies[way][0].start()

    def forward(self, s):
        for way in (0, 1):
            count = self.split[way]
            if s < count:
                self.copies[way][s].wait_recv()
                if s + 1 < count:
                    self.fill(way, s + 1)
                    self.copies[way][s + 1].start()

    def entry(self, k):
        rights, lefts = self.split
        item = self.lists[self.group_at(self.pos), k]
        value = self.table[self.index_of(item)]
        ahead = lax.rem(self.place_of(item) - self.pos + self.n, self.n)
        if rights > 0:
            value = jnp.where(ahead > lefts, self.slots[rights, k], value)
        if lefts > 0:
            value = jnp.where((ahead > 0) & (ahead <= lefts), self.slots[rights + 1 + lefts, k], value)
        return value

    def finish(self):
        for way in (0, 1):
            for copy in self.copies[way]:
                copy.wait_send()


def fetch_kernel(
    ny, nz, ntp,
    page_list, adapter_list, ids_ref, entries_ref, x_ref, k_ref, v_ref, cache_ref, down_ref, up_ref,
    lowrank_ref, up_out, kpage_out, vpage_out, kprev_out, vprev_out, code_out, idprev_out,
    down_tab, up_tab, kpage_tab, vpage_tab,
    down_slots, up_slots, kpage_slots, vpage_slots,
    down_all, parts, arrived,
    gather_send, gather_recv, slot_send, slot_recv, prev_send, prev_recv, sum_send, sum_recv, all_send, all_recv,
):
    group = lax.axis_index("grp")
    tp = lax.axis_index("tp")
    groups = ny * nz
    y, z = lax.div(group, nz), lax.rem(group, nz)
    z_right = (y * nz + lax.rem(z + 1, nz), tp)
    z_left = (y * nz + lax.rem(z + nz - 1, nz), tp)
    y_right = (lax.rem(y + 1, ny) * nz + z, tp)
    y_left = (lax.rem(y + ny - 1, ny) * nz + z, tp)
    after = (lax.rem(group + 1, groups), tp)
    before = (lax.rem(group + groups - 1, groups), tp)

    barrier = pltpu.get_barrier_semaphore()
    others = [(group, lax.rem(tp + d, ntp)) for d in range(1, ntp)]
    greeted = [z_right, z_left, y_right, y_left, after, before] + others
    for peer in greeted:
        pl.semaphore_signal(barrier, inc=1, device_id=peer, device_id_type=MESH)

    stored = down_ref.shape[0]
    for n in range(stored):
        down_tab[z, n] = down_ref[n]
        up_tab[y, n] = up_ref[n]
        kpage_tab[z, n] = cache_ref[n, 0]
        vpage_tab[y, n] = cache_ref[n, 1]

    pl.semaphore_wait(barrier, len(greeted))

    zs, ys = ring_split(nz, False), ring_split(ny, True)
    gathers = [
        Gather(down_tab, z, nz, z_right, z_left, zs, gather_send.at[0], gather_recv.at[0]),
        Gather(up_tab, y, ny, y_right, y_left, ys, gather_send.at[1], gather_recv.at[1]),
        Gather(kpage_tab, z, nz, z_right, z_left, zs, gather_send.at[2], gather_recv.at[2]),
        Gather(vpage_tab, y, ny, y_right, y_left, ys, gather_send.at[3], gather_recv.at[3]),
    ]

    def along_y(table, lists, slots, at):
        return Slots(
            table, lists, slots, y, ny, y_right, y_left, ys, slot_send.at[at], slot_recv.at[at],
            lambda target: target * nz + z,
            lambda item: (lax.rem(lax.div(item, stored), nz), lax.rem(item, stored)),
            lambda item: lax.div(item, stored * nz),
        )

    def along_z(table, lists, slots, at):
        return Slots(
            table, lists, slots, z, nz, z_right, z_left, zs, slot_send.at[at], slot_recv.at[at],
            lambda target: y * nz + target,
            lambda item: (lax.div(item, stored * nz), lax.rem(item, stored)),
            lambda item: lax.rem(lax.div(item, stored), nz),
        )

    adapters = [along_y(down_tab, adapter_list, down_slots, 0), along_z(up_tab, adapter_list, up_slots, 1)]
    pages = [along_y(kpage_tab, page_list, kpage_slots, 2), along_z(vpage_tab, page_list, vpage_slots, 3)]

    def prev_copy(src, dst, at):
        return pltpu.make_async_remote_copy(
            src_ref=src, dst_ref=dst, send_sem=prev_send.at[at], recv_sem=prev_recv.at[at],
            device_id=after, device_id_type=MESH,
        )

    prevs = [prev_copy(ids_ref, idprev_out, 0), prev_copy(k_ref, kprev_out, 1), prev_copy(v_ref, vprev_out, 2)]

    for gather in gathers:
        gather.start(0)
    for copy in prevs:
        copy.start()

    chunks = ids_ref.shape[0]
    code_columns = as_columns(entries_ref[...])
    for c in range(chunks):
        code_out[pl.ds(c, 1), :] = token_codes(ids_ref[pl.ds(c, 1), :], code_columns)

    for s in range(max(g.steps for g in gathers)):
        for gather in gathers:
            if s < gather.steps:
                gather.forward(s)

    for ring in adapters + pages:
        ring.start()
    for s in range(max(ring.steps for ring in adapters)):
        for ring in adapters:
            if s < ring.steps:
                ring.forward(s)
        if s == 0:
            for ring in pages:
                ring.forward(0)

    rank = down_ref.shape[1]
    listed = adapter_list.shape[1]
    for k in range(listed):
        down_all[k * rank:(k + 1) * rank, :] = adapters[0].entry(k)
        up_out[k] = adapters[1].entry(k)
    partial = lax.dot_general(
        down_all[...], x_ref[...], (((1,), (1,)), ((), ())), preferred_element_type=F32
    )
    for c in range(chunks):
        entry = lax.rem(code_out[pl.ds(c, 1), :], listed)
        total = jnp.zeros((rank, BLOCK), F32)
        for k in range(listed):
            total = jnp.where(entry == k, partial[k * rank:(k + 1) * rank, c * BLOCK:(c + 1) * BLOCK], total)
        parts[c] = total

    each = chunks // ntp
    sums = []
    for d in range(1, ntp):
        peer = lax.rem(tp + d, ntp)
        copy = pltpu.make_async_remote_copy(
            src_ref=parts.at[pl.ds(peer * each, each)], dst_ref=arrived.at[d - 1],
            send_sem=sum_send.at[d - 1], recv_sem=sum_recv.at[d - 1],
            device_id=(group, peer), device_id_type=MESH,
        )
        copy.start()
        sums.append(copy)

    for ring in pages:
        if ring.steps > 1:
            ring.forward(1)

    total = parts[pl.ds(tp * each, each)]
    for d, copy in enumerate(sums):
        copy.wait_recv()
        total = total + arrived[d]
    lowrank_ref[pl.ds(tp * each, each)] = total.astype(BF16)
    spread = []
    for d in range(1, ntp):
        copy = pltpu.make_async_remote_copy(
            src_ref=lowrank_ref.at[pl.ds(tp * each, each)], dst_ref=lowrank_ref.at[pl.ds(tp * each, each)],
            send_sem=all_send.at[d - 1], recv_sem=all_recv.at[d - 1],
            device_id=(group, lax.rem(tp + d, ntp)), device_id_type=MESH,
        )
        copy.start()
        spread.append(copy)

    for s in range(2, max(ring.steps for ring in pages)):
        for ring in pages:
            if s < ring.steps:
                ring.forward(s)
    for k in range(page_list.shape[1]):
        kpage_out[pl.ds(k * PAGE, PAGE), :] = pages[0].entry(k)
        vpage_out[pl.ds(k * PAGE, PAGE), :] = pages[1].entry(k)

    for copy in spread + prevs:
        copy.wait_recv()
    for copy in sums + spread + prevs:
        copy.wait_send()
    for ring in gathers + adapters + pages:
        ring.finish()


def attend_kernel(
    q_ref, lowrank_ref, up_ref, kpage_ref, vpage_ref, kprev_ref, vprev_ref, k_ref, v_ref, code_ref, ids_ref, idprev_ref,
    out_ref, keys, values, key_ids,
):
    i = pl.program_id(0)
    tokens = k_ref.shape[0]
    chunks = tokens // BLOCK

    @pl.when(i == 0)
    def _():
        first = lax.axis_index("grp") == 0
        keys[:tokens, :] = kprev_ref[...]
        keys[tokens:, :] = k_ref[...]
        values[:tokens, :] = vprev_ref[...]
        values[tokens:, :] = v_ref[...]
        key_ids[:chunks, :] = jnp.where(first, -1, idprev_ref[...])
        key_ids[chunks:, :] = ids_ref[...]

    listed = up_ref.shape[0]
    code = code_ref[pl.ds(i, 1), :]
    entry = lax.rem(code, listed)
    low = lowrank_ref[0]
    wide = jnp.concatenate([jnp.where(entry == k, low, jnp.zeros_like(low)) for k in range(listed)], axis=0)
    up_all = jnp.concatenate([up_ref[k] for k in range(listed)], axis=0)
    update = lax.dot_general(wide, up_all, (((0,), (0,)), ((), ())), preferred_element_type=F32)
    query = (q_ref[...].astype(F32) + ADAPTER_SCALE * update).astype(BF16)

    page_of = as_columns(lax.div(code, listed))
    ids = as_columns(ids_ref[pl.ds(i, 1), :])
    start = pl.multiple_of(i * BLOCK, BLOCK)
    band = tokens + BLOCK
    kband = keys[pl.ds(start, band), :]
    vband = values[pl.ds(start, band), :]
    row = lax.broadcasted_iota(jnp.int32, (BLOCK, BLOCK), 0)
    column = lax.broadcasted_iota(jnp.int32, (BLOCK, BLOCK), 1)
    masks = []
    for c in range(chunks + 1):
        mask = ids == key_ids[pl.ds(i + c, 1), :]
        if c == chunks:
            mask = mask & (column <= row)
        masks.append(mask)
    npages = kpage_ref.shape[0] // PAGE
    for k in range(npages):
        masks.append(page_of == k)
    factor = math.log2(math.e) * HEAD_WIDTH ** -0.5
    nt = (((1,), (1,)), ((), ()))
    for h in range(PER_KV):
        qh = query[:, h * HEAD_WIDTH:(h + 1) * HEAD_WIDTH]
        sb = lax.dot_general(qh, kband, nt, preferred_element_type=F32)
        sp = lax.dot_general(qh, kpage_ref[...], nt, preferred_element_type=F32)
        pieces = [sb[:, c * BLOCK:(c + 1) * BLOCK] for c in range(chunks + 1)]
        pieces += [sp[:, c * PAGE:(c + 1) * PAGE] for c in range(npages)]
        pieces = [jnp.where(mask, piece, F32(-1e30)) for mask, piece in zip(masks, pieces)]
        top = functools.reduce(jnp.maximum, pieces)
        top = jnp.max(top, axis=1, keepdims=True)
        expos = [jnp.exp2((piece - top) * factor) for piece in pieces]
        total = jnp.sum(functools.reduce(jnp.add, expos), axis=1, keepdims=True)
        weights = [e.astype(BF16) for e in expos]
        mixed = jnp.dot(jnp.concatenate(weights[:chunks + 1], axis=1), vband, preferred_element_type=F32)
        mixed += jnp.dot(jnp.concatenate(weights[chunks + 1:], axis=1), vpage_ref[...], preferred_element_type=F32)
        out_ref[:, h * HEAD_WIDTH:(h + 1) * HEAD_WIDTH] = (mixed / total).astype(BF16)


def fetch(ny, nz, ntp, page_list, adapter_list, ids, entries, x, k, v, cache, down, up):
    chunks = ids.shape[0]
    stored, rank, features = down.shape
    listed, plisted = adapter_list.shape[1], page_list.shape[1]
    page_rows = plisted * PAGE
    struct = jax.ShapeDtypeStruct
    vmem = pl.BlockSpec(memory_space=pltpu.VMEM)
    smem = pl.BlockSpec(memory_space=pltpu.SMEM)
    anywhere = pl.BlockSpec(memory_space=pl.ANY)
    most = max(ny, nz) - 1
    each = chunks // ntp
    dma = pltpu.SemaphoreType.DMA
    return pl.pallas_call(
        functools.partial(fetch_kernel, ny, nz, ntp),
        out_shape=(
            struct((chunks, rank, BLOCK), BF16),
            struct((listed, rank, features), BF16),
            struct((page_rows, HEAD_WIDTH), BF16),
            struct((page_rows, HEAD_WIDTH), BF16),
            struct(k.shape, BF16),
            struct(v.shape, BF16),
            struct(ids.shape, jnp.int32),
            struct(ids.shape, jnp.int32),
        ),
        in_specs=[smem, smem, vmem, vmem, vmem, vmem, vmem, vmem, vmem, vmem],
        out_specs=(vmem,) * 8,
        scratch_shapes=[
            pltpu.VMEM((nz, stored, rank, features), BF16),
            pltpu.VMEM((ny, stored, rank, features), BF16),
            pltpu.VMEM((nz, stored, PAGE, HEAD_WIDTH), BF16),
            pltpu.VMEM((ny, stored, PAGE, HEAD_WIDTH), BF16),
            pltpu.VMEM((ny + 1, listed, rank, features), BF16),
            pltpu.VMEM((nz + 1, listed, rank, features), BF16),
            pltpu.VMEM((ny + 1, plisted, PAGE, HEAD_WIDTH), BF16),
            pltpu.VMEM((nz + 1, plisted, PAGE, HEAD_WIDTH), BF16),
            pltpu.VMEM((listed * rank, features), BF16),
            pltpu.VMEM((chunks, rank, BLOCK), F32),
            pltpu.VMEM((max(ntp - 1, 1), each, rank, BLOCK), F32),
            dma((4, most)), dma((4, most)), dma((4, most)), dma((4, most)),
            dma((3,)), dma((3,)),
            dma((max(ntp - 1, 1),)), dma((max(ntp - 1, 1),)), dma((max(ntp - 1, 1),)), dma((max(ntp - 1, 1),)),
        ],
        compiler_params=pltpu.CompilerParams(
            collective_id=0, has_side_effects=True, vmem_limit_bytes=40 * 1024 * 1024
        ),
        name="fetch",
    )(page_list, adapter_list, ids, entries, x, k, v, cache, down, up)


def attend(q, lowrank, up, kpage, vpage, kprev, vprev, k, v, code, ids, idprev):
    tokens, width = q.shape
    rank = lowrank.shape[1]
    whole = lambda a: pl.BlockSpec(a.shape, lambda i: (0,) * a.ndim)
    return pl.pallas_call(
        attend_kernel,
        grid=(tokens // BLOCK,),
        out_shape=jax.ShapeDtypeStruct(q.shape, BF16),
        in_specs=[
            pl.BlockSpec((BLOCK, width), lambda i: (i, 0)),
            pl.BlockSpec((1, rank, BLOCK), lambda i: (i, 0, 0)),
        ] + [whole(a) for a in (up, kpage, vpage, kprev, vprev, k, v, code, ids, idprev)],
        out_specs=pl.BlockSpec((BLOCK, width), lambda i: (i, 0)),
        scratch_shapes=[
            pltpu.VMEM((2 * tokens, HEAD_WIDTH), BF16),
            pltpu.VMEM((2 * tokens, HEAD_WIDTH), BF16),
            pltpu.VMEM((2 * tokens // BLOCK, BLOCK), jnp.int32),
        ],
        compiler_params=pltpu.CompilerParams(vmem_limit_bytes=40 * 1024 * 1024),
        name="attend",
    )(q, lowrank, up, kpage, vpage, kprev, vprev, k, v, code, ids, idprev)


def solution(mesh, nz=8):
    groups, ntp = mesh.shape["grp"], mesh.shape["tp"]
    ny = groups // nz

    def local(x, q, k, v, request, cache, down, up, page_list, adapter_list, page_entry, adapter_entry):
        listed = adapter_list.shape[1]
        ids = request.reshape(-1, BLOCK)
        entries = (page_entry * listed + adapter_entry).reshape(1, -1)
        lowrank, up_own, kpage, vpage, kprev, vprev, code, idprev = fetch(
            ny, nz, ntp, page_list, adapter_list, ids, entries, x, k, v, cache, down, up
        )
        return attend(q, lowrank, up_own, kpage, vpage, kprev, vprev, k, v, code, ids, idprev)

    placed = (
        P("grp", "tp"),
        P("grp", "tp"),
        P("grp", "tp"),
        P("grp", "tp"),
        P("grp"),
        P("grp", None, None, "tp"),
        P("grp", None, "tp"),
        P("grp", None, "tp"),
        P(),
        P(),
        P(),
        P(),
    )
    return jax.shard_map(local, mesh=mesh, in_specs=placed, out_specs=P("grp", "tp"), check_vma=False)
```

```python
import functools
import math

import jax
import jax.numpy as jnp
from jax import lax
from jax.experimental import pallas as pl
from jax.experimental.pallas import tpu as pltpu
from jax.sharding import PartitionSpec as P

PER_KV = 4
HEAD_WIDTH = 128
PAGE = 128
BLOCK = 128
ADAPTER_SCALE = 0.5
MESH = pl.DeviceIdType.MESH
F32 = jnp.float32
BF16 = jnp.bfloat16


def ring_split(n, heavy_right):
    more, fewer = n // 2, (n - 1) // 2
    return (more, fewer) if heavy_right else (fewer, more)


def token_codes(ids_row, table_columns):
    requests = table_columns.shape[0]
    numbers = lax.broadcasted_iota(jnp.int32, (requests, ids_row.shape[1]), 0)
    return jnp.sum(jnp.where(numbers == ids_row, table_columns, 0), axis=0, keepdims=True)


def as_columns(row):
    return jnp.broadcast_to(row, (128, row.shape[1])).T


class Gather:
    def __init__(self, table, pos, n, peers, split, send, recv):
        self.copies = []
        for s in range(1, max(split) + 1):
            now = []
            for way in (0, 1):
                if s <= split[way]:
                    origin = lax.rem(pos - (s - 1) + n, n) if way == 0 else lax.rem(pos + (s - 1), n)
                    at = s - 1 if way == 0 else split[0] + s - 1
                    now.append(remote(table.at[origin], table.at[origin], send.at[at], recv.at[at], peers[way]))
                else:
                    now.append(None)
            self.copies.append(now)
        self.steps = len(self.copies)

    def start(self):
        for copy in self.copies[0]:
            if copy is not None:
                copy.start()

    def forward(self, s):
        for way, copy in enumerate(self.copies[s]):
            if copy is not None:
                copy.wait_recv()
                if s + 1 < self.steps and self.copies[s + 1][way] is not None:
                    self.copies[s + 1][way].start()

    def finish(self):
        for now in self.copies:
            for copy in now:
                if copy is not None:
                    copy.wait_send()


class Slots:
    def __init__(self, load, lists, picks, slots, pos, n, peers, split, send, recv, group_at, index_of, place_of):
        self.load, self.lists, self.picks, self.slots, self.pos, self.n = load, lists, picks, slots, pos, n
        self.split = split
        self.base = (0, split[0] + 1)
        self.group_at, self.index_of, self.place_of = group_at, index_of, place_of
        self.copies = []
        for way in (0, 1):
            base = self.base[way]
            sems = 0 if way == 0 else split[0]
            self.copies.append(
                [
                    remote(slots.at[base + s], slots.at[base + s + 1], send.at[sems + s], recv.at[sems + s], peers[way])
                    for s in range(split[way])
                ]
            )
        self.steps = max(split)
        self.plan = {}

    def prepare(self):
        for way in (0, 1):
            for s in range(self.split[way] + 1):
                away = self.split[way] - s
                target = lax.rem(self.pos + away, self.n) if way == 0 else lax.rem(self.pos - away + self.n, self.n)
                group = self.group_at(target)
                items = [self.lists[k, group] for k in self.picks]
                self.plan[way, s] = [(self.index_of(item), self.place_of(item)) for item in items]

    def fill(self, way, s, wait=None):
        plan = self.plan[way, s]
        mine = [self.load(index) for index, _ in plan]
        if wait is not None:
            wait()
        at = self.base[way] + s
        for k, (_, place) in enumerate(plan):
            value = mine[k]
            if s > 0:
                value = jnp.where(place == self.pos, value, self.slots[at, k])
            self.slots[at, k] = value

    def start(self):
        for way in (0, 1):
            if self.split[way] > 0:
                self.fill(way, 0)
                self.copies[way][0].start()

    def forward(self, s):
        for way in (0, 1):
            if s < self.split[way]:
                copy = self.copies[way][s]
                if s + 1 < self.split[way]:
                    self.fill(way, s + 1, copy.wait_recv)
                    self.copies[way][s + 1].start()
                else:
                    copy.wait_recv()

    def entry(self, k):
        rights, lefts = self.split
        index, place = self.plan[0, rights][k]
        value = self.load(index)
        ahead = lax.rem(place - self.pos + self.n, self.n)
        if rights > 0:
            value = jnp.where(ahead > lefts, self.slots[rights, k], value)
        if lefts > 0:
            value = jnp.where((ahead > 0) & (ahead <= lefts), self.slots[rights + 1 + lefts, k], value)
        return value

    def finish(self):
        for way in (0, 1):
            for copy in self.copies[way]:
                copy.wait_send()


def remote(src, dst, send, recv, peer):
    return pltpu.make_async_remote_copy(
        src_ref=src, dst_ref=dst, send_sem=send, recv_sem=recv, device_id=peer, device_id_type=MESH
    )


PREV_PARTS = 4
FACTOR = math.log2(math.e) * HEAD_WIDTH ** -0.5
NT = (((1,), (1,)), ((), ()))
TN = (((0,), (0,)), ((), ()))


def fused_kernel(
    ny, nz, ntp,
    page_list, adapter_list, page_entry_ref, adapter_entry_ref,
    ids_hbm, x_hbm, q_hbm, k_hbm, v_hbm, cache_hbm, down_hbm, up_hbm,
    out_hbm,
    down_tab, up_tab, kpage_tab, vpage_tab,
    down_slots, up_slots, kpage_slots, vpage_slots,
    x_ref, q_ref, ids_ref, idprev_ref, code_ref, down_all, up_all,
    keys, values, values_t, key_ids, kpages, vpages_t,
    parts, from_pair, half_sum, from_x, lowrank_ref,
    queries, tops, sums_ref, mixed_ref, out_ref,
    gather_send, gather_recv, slot_send, slot_recv, prev_send, prev_recv, pair_send, pair_recv, x_send, x_recv,
    here, done,
):
    group = lax.axis_index("grp")
    tp = lax.axis_index("tp")
    groups = ny * nz
    y, z = lax.div(group, nz), lax.rem(group, nz)
    z_peers = ((y * nz + lax.rem(z + 1, nz), tp), (y * nz + lax.rem(z + nz - 1, nz), tp))
    y_peers = ((lax.rem(y + 1, ny) * nz + z, tp), (lax.rem(y + ny - 1, ny) * nz + z, tp))
    after = (lax.rem(group + 1, groups), tp)
    before = (lax.rem(group + groups - 1, groups), tp)
    core = lax.rem(tp, 2)
    pair = (group, tp + 1 - 2 * core)
    x_peers = [(group, lax.rem(tp + 2 * d, ntp)) for d in range(1, ntp // 2)]

    barrier = pltpu.get_barrier_semaphore()
    greeted = [z_peers[0], z_peers[1], y_peers[0], y_peers[1], after, before, pair] + x_peers
    for peer in greeted:
        pl.semaphore_signal(barrier, inc=1, device_id=peer, device_id_type=MESH)

    stored, rank = down_hbm.shape[0], down_hbm.shape[1]
    tokens = k_hbm.shape[0]
    chunks = tokens // BLOCK
    listed, plisted = adapter_list.shape[0], page_list.shape[0]
    half = plisted // 2

    own = [
        pltpu.make_async_copy(down_hbm, down_tab.at[z], here.at[0]),
        pltpu.make_async_copy(up_hbm, up_tab.at[y], here.at[1]),
        pltpu.make_async_copy(cache_hbm.at[:, 0], kpage_tab.at[z], here.at[2]),
        pltpu.make_async_copy(cache_hbm.at[:, 1], vpage_tab.at[y], here.at[3]),
    ]
    own_rows = pl.ds(tokens, tokens)
    staged = [
        pltpu.make_async_copy(ids_hbm, ids_ref, here.at[4]),
        pltpu.make_async_copy(x_hbm, x_ref, here.at[5]),
        pltpu.make_async_copy(q_hbm, q_ref, here.at[6]),
        pltpu.make_async_copy(k_hbm, keys.at[own_rows], here.at[7]),
        pltpu.make_async_copy(v_hbm, values.at[own_rows], here.at[8]),
    ]
    for copy in own + staged:
        copy.start()

    zs, ys = ring_split(nz, False), ring_split(ny, True)
    gathers = [
        Gather(down_tab, z, nz, z_peers, zs, gather_send.at[0], gather_recv.at[0]),
        Gather(up_tab, y, ny, y_peers, ys, gather_send.at[1], gather_recv.at[1]),
        Gather(kpage_tab, z, nz, z_peers, zs, gather_send.at[2], gather_recv.at[2]),
        Gather(vpage_tab, y, ny, y_peers, ys, gather_send.at[3], gather_recv.at[3]),
    ]

    def along_y(table, lists, picks, slots, at):
        return Slots(
            lambda index: table[index], lists, picks, slots, y, ny, y_peers, ys, slot_send.at[at], slot_recv.at[at],
            lambda target: target * nz + z,
            lambda item: (lax.rem(lax.div(item, stored), nz), lax.rem(item, stored)),
            lambda item: lax.div(item, stored * nz),
        )

    def along_z(table, lists, picks, slots, at):
        return Slots(
            lambda index: table[index], lists, picks, slots, z, nz, z_peers, zs, slot_send.at[at], slot_recv.at[at],
            lambda target: y * nz + target,
            lambda item: (lax.div(item, stored * nz), lax.rem(item, stored)),
            lambda item: lax.rem(lax.div(item, stored), nz),
        )

    downs = along_y(down_tab, adapter_list, range(listed), down_slots, 0)
    ups = along_z(up_tab, adapter_list, range(listed), up_slots, 1)
    pages = [
        ring
        for part in range(2)
        for ring in (
            along_y(kpage_tab, page_list, range(part * half, part * half + half), kpage_slots.at[part], 2 + part),
            along_z(vpage_tab, page_list, range(part * half, part * half + half), vpage_slots.at[part], 4 + part),
        )
    ]

    rows = tokens // PREV_PARTS
    prevs = []
    for part in range(PREV_PARTS):
        at = pl.ds(part * rows, rows)
        prevs.append(remote(k_hbm.at[at], keys.at[at], prev_send.at[0, part], prev_recv.at[0, part], after))
        prevs.append(remote(v_hbm.at[at], values.at[at], prev_send.at[1, part], prev_recv.at[1, part], after))
    idprev = remote(ids_hbm, idprev_ref, prev_send.at[2, 0], prev_recv.at[2, 0], after)
    waiting = list(prevs)

    def some_prev(count):
        for _ in range(min(count, len(waiting))):
            waiting.pop(0).start()

    pl.semaphore_wait(barrier, len(greeted))
    for copy, gather in zip(own, gathers):
        copy.wait()
        gather.start()
    idprev.start()
    some_prev(1)

    for ring in [downs, ups] + pages:
        ring.prepare()
    staged[0].wait()
    code_columns = as_columns(page_entry_ref[...] * listed + adapter_entry_ref[...])
    for c in range(chunks):
        code_ref[pl.ds(c, 1), :] = token_codes(ids_ref[pl.ds(c, 1), :], code_columns)
        key_ids[pl.ds(tokens + c * BLOCK, BLOCK), :] = as_columns(ids_ref[pl.ds(c, 1), :])

    gsteps = max(g.steps for g in gathers)

    def gather_step(which, s):
        for gather in which:
            if 0 <= s < gather.steps:
                gather.forward(s)

    def slot_step(which, s):
        for ring in which:
            if 0 <= s < ring.steps:
                ring.forward(s)

    for s in range(gsteps):
        gather_step(gathers[:2], s)
        gather_step(gathers[2:], s - 1)
        some_prev(1)
    downs.start()
    ups.start()
    gather_step(gathers[2:], gsteps - 1)
    slot_step([downs], 0)
    for ring in pages:
        ring.start()
    slot_step([ups], 0)
    steps = max(downs.steps, ups.steps)
    for s in range(1, steps):
        slot_step([downs], s)
        slot_step([ups], s)
        if s + 1 < steps:
            slot_step(pages, s - 1)
        some_prev(2)
    some_prev(len(waiting))
    served = max(steps - 2, 0)

    for k in range(listed):
        down_all[k * rank:(k + 1) * rank, :] = downs.entry(k)
    staged[1].wait()
    partial = lax.dot_general(down_all[...], x_ref[...], NT, preferred_element_type=F32)
    for c in range(chunks):
        entry = lax.rem(code_ref[pl.ds(c, 1), :], listed)
        total = jnp.zeros((rank, BLOCK), F32)
        for k in range(listed):
            total = jnp.where(entry == k, partial[k * rank:(k + 1) * rank, c * BLOCK:(c + 1) * BLOCK], total)
        parts[c] = total
    each = chunks // 2
    mine = pl.ds(core * each, each)
    theirs = pl.ds((1 - core) * each, each)
    to_pair = remote(parts.at[theirs], from_pair, pair_send.at[0], pair_recv.at[0], pair)
    to_pair.start()
    to_pair.wait_recv()
    half_sum[...] = parts[mine] + from_pair[...]
    to_x = [
        remote(half_sum, from_x.at[d], x_send.at[d], x_recv.at[d], peer) for d, peer in enumerate(x_peers)
    ]
    for copy in to_x:
        copy.start()

    for k in range(listed):
        up_all[k * rank:(k + 1) * rank, :] = ups.entry(k)
    for copy in staged[2:]:
        copy.wait()
    for c in range(chunks):
        at = tokens + c * BLOCK
        values_t[:, at:at + BLOCK] = values[at:at + BLOCK, :].T
    if served + 1 < steps:
        slot_step(pages, served)
        served += 1
    for copy in prevs + [idprev]:
        copy.wait_recv()
    first = group == 0
    for c in range(chunks):
        at = c * BLOCK
        values_t[:, at:at + BLOCK] = values[at:at + BLOCK, :].T
        key_ids[at:at + BLOCK, :] = as_columns(jnp.where(first, -1, idprev_ref[pl.ds(c, 1), :]))

    total = half_sum[...]
    for d, copy in enumerate(to_x):
        copy.wait_recv()
        total = total + from_x[d]
    lowrank_ref[mine] = total.astype(BF16)
    back = remote(lowrank_ref.at[mine], lowrank_ref.at[mine], pair_send.at[1], pair_recv.at[1], pair)
    back.start()
    back.wait_recv()

    band = tokens + BLOCK
    later = lax.broadcasted_iota(jnp.int32, (BLOCK, BLOCK), 0)
    sooner = lax.broadcasted_iota(jnp.int32, (BLOCK, BLOCK), 1)
    causal = later <= sooner

    def band_block(i, carry):
        start = pl.multiple_of(i * BLOCK, BLOCK)
        entry = lax.rem(code_ref[pl.ds(i, 1), :], listed)
        low = lowrank_ref[i]
        wide = jnp.concatenate([jnp.where(entry == k, low, jnp.zeros_like(low)) for k in range(listed)], axis=0)
        update = lax.dot_general(wide, up_all[...], TN, preferred_element_type=F32)
        query = (q_ref[pl.ds(start, BLOCK), :].astype(F32) + ADAPTER_SCALE * update).astype(BF16)
        stacked = jnp.concatenate([query[:, h * HEAD_WIDTH:(h + 1) * HEAD_WIDTH] for h in range(PER_KV)], axis=0)
        queries[i] = stacked
        scores = lax.dot_general(keys[pl.ds(start, band), :], stacked, NT, preferred_element_type=F32)
        ids_row = ids_ref[pl.ds(i, 1), :]
        masks = [key_ids[pl.ds(start + c * BLOCK, BLOCK), :] == ids_row for c in range(chunks + 1)]
        masks[chunks] = masks[chunks] & causal
        weights = []
        for h in range(PER_KV):
            across = slice(h * BLOCK, (h + 1) * BLOCK)
            pieces = [
                jnp.where(masks[c], scores[c * BLOCK:(c + 1) * BLOCK, across], F32(-1e30)) for c in range(chunks + 1)
            ]
            top = jnp.max(functools.reduce(jnp.maximum, pieces), axis=0, keepdims=True)
            expos = [jnp.exp2((piece - top) * FACTOR) for piece in pieces]
            tops[i, h:h + 1, :] = top
            sums_ref[i, h:h + 1, :] = jnp.sum(functools.reduce(jnp.add, expos), axis=0, keepdims=True)
            weights.append(jnp.concatenate([e.astype(BF16) for e in expos], axis=0))
        mixed_ref[i] = jnp.dot(
            values_t[:, pl.ds(start, band)], jnp.concatenate(weights, axis=1), preferred_element_type=F32
        )
        return carry

    while served + 1 < steps:
        slot_step(pages, served)
        served += 1
    lax.fori_loop(0, chunks, band_block, 0, unroll=2)
    slot_step(pages, served)

    for part in range(2):
        for k in range(half):
            at = (part * half + k) * PAGE
            kpages[at:at + PAGE, :] = pages[2 * part].entry(k)
            vpages_t[:, at:at + PAGE] = pages[2 * part + 1].entry(k).T

    def page_block(i, carry):
        start = pl.multiple_of(i * BLOCK, BLOCK)
        scores = lax.dot_general(kpages[...], queries[i], NT, preferred_element_type=F32)
        page_of = lax.div(code_ref[pl.ds(i, 1), :], listed)
        weights, scales = [], []
        for h in range(PER_KV):
            across = slice(h * BLOCK, (h + 1) * BLOCK)
            piece = scores[:PAGE, across]
            for k in range(1, plisted):
                piece = jnp.where(page_of == k, scores[k * PAGE:(k + 1) * PAGE, across], piece)
            before_top = tops[i, h:h + 1, :]
            top = jnp.maximum(jnp.max(piece, axis=0, keepdims=True), before_top)
            expo = jnp.exp2((piece - top) * FACTOR)
            shrink = jnp.exp2((before_top - top) * FACTOR)
            total = sums_ref[i, h:h + 1, :] * shrink + jnp.sum(expo, axis=0, keepdims=True)
            scales.append((shrink, 1.0 / total))
            weights.append(
                jnp.concatenate([jnp.where(page_of == k, expo, 0.0).astype(BF16) for k in range(plisted)], axis=0)
            )
        mixed = jnp.dot(vpages_t[...], jnp.concatenate(weights, axis=1), preferred_element_type=F32)
        for h in range(PER_KV):
            across = slice(h * BLOCK, (h + 1) * BLOCK)
            shrink, inverse = scales[h]
            value = (mixed_ref[i, :, across] * shrink + mixed[:, across]) * inverse
            out_ref[pl.ds(start, BLOCK), h * HEAD_WIDTH:(h + 1) * HEAD_WIDTH] = value.T.astype(BF16)
        at = pl.ds(start, BLOCK)
        pltpu.make_async_copy(out_ref.at[at], out_hbm.at[at], done.at[i]).start()
        return carry

    lax.fori_loop(0, chunks, page_block, 0, unroll=2)

    for copy in prevs + [idprev, to_pair, back] + to_x:
        copy.wait_send()
    for ring in gathers + [downs, ups] + pages:
        ring.finish()
    for i in range(chunks):
        at = pl.ds(i * BLOCK, BLOCK)
        pltpu.make_async_copy(out_ref.at[at], out_hbm.at[at], done.at[i]).wait()


def fused(ny, nz, ntp, page_list, adapter_list, page_entry, adapter_entry, ids, x, q, k, v, cache, down, up):
    chunks = ids.shape[0]
    tokens = k.shape[0]
    stored, rank, features = down.shape
    listed, plisted = adapter_list.shape[0], page_list.shape[0]
    half = plisted // 2
    vmem = pl.BlockSpec(memory_space=pltpu.VMEM)
    smem = pl.BlockSpec(memory_space=pltpu.SMEM)
    hbm = pl.BlockSpec(memory_space=pltpu.HBM)
    most = max(ny, nz) - 1
    nx = max(ntp // 2 - 1, 1)
    dma = pltpu.SemaphoreType.DMA
    stack = PER_KV * BLOCK
    return pl.pallas_call(
        functools.partial(fused_kernel, ny, nz, ntp),
        out_shape=jax.ShapeDtypeStruct(q.shape, BF16),
        in_specs=[smem, smem, vmem, vmem] + [hbm] * 8,
        out_specs=hbm,
        scratch_shapes=[
            pltpu.VMEM((nz, stored, rank, features), BF16),
            pltpu.VMEM((ny, stored, rank, features), BF16),
            pltpu.VMEM((nz, stored, PAGE, HEAD_WIDTH), BF16),
            pltpu.VMEM((ny, stored, PAGE, HEAD_WIDTH), BF16),
            pltpu.VMEM((ny + 1, listed, rank, features), BF16),
            pltpu.VMEM((nz + 1, listed, rank, features), BF16),
            pltpu.VMEM((2, ny + 1, half, PAGE, HEAD_WIDTH), BF16),
            pltpu.VMEM((2, nz + 1, half, PAGE, HEAD_WIDTH), BF16),
            pltpu.VMEM(x.shape, BF16),
            pltpu.VMEM(q.shape, BF16),
            pltpu.VMEM(ids.shape, jnp.int32),
            pltpu.VMEM(ids.shape, jnp.int32),
            pltpu.VMEM(ids.shape, jnp.int32),
            pltpu.VMEM((listed * rank, features), BF16),
            pltpu.VMEM((listed * rank, features), BF16),
            pltpu.VMEM((2 * tokens, HEAD_WIDTH), BF16),
            pltpu.VMEM((2 * tokens, HEAD_WIDTH), BF16),
            pltpu.VMEM((HEAD_WIDTH, 2 * tokens), BF16),
            pltpu.VMEM((2 * tokens, BLOCK), jnp.int32),
            pltpu.VMEM((plisted * PAGE, HEAD_WIDTH), BF16),
            pltpu.VMEM((HEAD_WIDTH, plisted * PAGE), BF16),
            pltpu.VMEM((chunks, rank, BLOCK), F32),
            pltpu.VMEM((chunks // 2, rank, BLOCK), F32),
            pltpu.VMEM((chunks // 2, rank, BLOCK), F32),
            pltpu.VMEM((nx, chunks // 2, rank, BLOCK), F32),
            pltpu.VMEM((chunks, rank, BLOCK), BF16),
            pltpu.VMEM((chunks, stack, HEAD_WIDTH), BF16),
            pltpu.VMEM((chunks, 8, BLOCK), F32),
            pltpu.VMEM((chunks, 8, BLOCK), F32),
            pltpu.VMEM((chunks, HEAD_WIDTH, stack), F32),
            pltpu.VMEM(q.shape, BF16),
            dma((4, most)), dma((4, most)), dma((6, most)), dma((6, most)),
            dma((3, PREV_PARTS)), dma((3, PREV_PARTS)),
            dma((2,)), dma((2,)), dma((nx,)), dma((nx,)),
            dma((9,)), dma((chunks,)),
        ],
        compiler_params=pltpu.CompilerParams(
            collective_id=0, has_side_effects=True, vmem_limit_bytes=56 * 1024 * 1024
        ),
        name="fused",
    )(page_list, adapter_list, page_entry, adapter_entry, ids, x, q, k, v, cache, down, up)


def solution(mesh, nz=8):
    groups, ntp = mesh.shape["grp"], mesh.shape["tp"]
    ny = groups // nz

    def local(x, q, k, v, request, cache, down, up, page_list, adapter_list, page_entry, adapter_entry):
        return fused(
            ny, nz, ntp, page_list.T, adapter_list.T, page_entry.reshape(1, -1), adapter_entry.reshape(1, -1),
            request.reshape(-1, BLOCK), x, q, k, v, cache, down, up,
        )

    placed = (
        P("grp", "tp"),
        P("grp", "tp"),
        P("grp", "tp"),
        P("grp", "tp"),
        P("grp"),
        P("grp", None, None, "tp"),
        P("grp", None, "tp"),
        P("grp", None, "tp"),
        P(),
        P(),
        P(),
        P(),
    )
    return jax.shard_map(local, mesh=mesh, in_specs=placed, out_specs=P("grp", "tp"), check_vma=False)
```

```python
import functools
import math

import jax
import jax.numpy as jnp
from jax import lax
from jax.experimental import pallas as pl
from jax.experimental.pallas import tpu as pltpu
from jax.sharding import PartitionSpec as P

PER_KV = 4
HEAD_WIDTH = 128
PAGE = 128
BLOCK = 128
ADAPTER_SCALE = 0.5
MESH = pl.DeviceIdType.MESH
F32 = jnp.float32
BF16 = jnp.bfloat16


def ring_split(n, heavy_right):
    more, fewer = n // 2, (n - 1) // 2
    return (more, fewer) if heavy_right else (fewer, more)


def token_codes(ids_row, table_columns):
    requests = table_columns.shape[0]
    numbers = lax.broadcasted_iota(jnp.int32, (requests, ids_row.shape[1]), 0)
    return jnp.sum(jnp.where(numbers == ids_row, table_columns, 0), axis=0, keepdims=True)


def as_columns(row):
    return jnp.broadcast_to(row, (128, row.shape[1])).T


class Gather:
    def __init__(self, table, pos, n, peers, split, send, recv):
        self.copies = []
        for s in range(1, max(split) + 1):
            now = []
            for way in (0, 1):
                if s <= split[way]:
                    origin = lax.rem(pos - (s - 1) + n, n) if way == 0 else lax.rem(pos + (s - 1), n)
                    at = s - 1 if way == 0 else split[0] + s - 1
                    now.append(remote(table.at[origin], table.at[origin], send.at[at], recv.at[at], peers[way]))
                else:
                    now.append(None)
            self.copies.append(now)
        self.steps = len(self.copies)

    def start(self):
        for copy in self.copies[0]:
            if copy is not None:
                copy.start()

    def forward(self, s):
        for way, copy in enumerate(self.copies[s]):
            if copy is not None:
                copy.wait_recv()
                if s + 1 < self.steps and self.copies[s + 1][way] is not None:
                    self.copies[s + 1][way].start()

    def finish(self):
        for now in self.copies:
            for copy in now:
                if copy is not None:
                    copy.wait_send()


class Slots:
    def __init__(self, load, lists, picks, slots, pos, n, peers, split, send, recv, group_at, index_of, place_of):
        self.load, self.lists, self.picks, self.slots, self.pos, self.n = load, lists, picks, slots, pos, n
        self.split = split
        self.base = (0, split[0] + 1)
        self.group_at, self.index_of, self.place_of = group_at, index_of, place_of
        self.copies = []
        for way in (0, 1):
            base = self.base[way]
            sems = 0 if way == 0 else split[0]
            self.copies.append(
                [
                    remote(slots.at[base + s], slots.at[base + s + 1], send.at[sems + s], recv.at[sems + s], peers[way])
                    for s in range(split[way])
                ]
            )
        self.steps = max(split)
        self.plan = {}

    def prepare(self):
        for way in (0, 1):
            for s in range(self.split[way] + 1):
                away = self.split[way] - s
                target = lax.rem(self.pos + away, self.n) if way == 0 else lax.rem(self.pos - away + self.n, self.n)
                group = self.group_at(target)
                items = [self.lists[k, group] for k in self.picks]
                self.plan[way, s] = [(self.index_of(item), self.place_of(item)) for item in items]

    def fill(self, way, s, wait=None):
        plan = self.plan[way, s]
        mine = [self.load(index) for index, _ in plan]
        if wait is not None:
            wait()
        at = self.base[way] + s
        for k, (_, place) in enumerate(plan):
            value = mine[k]
            if s > 0:
                value = jnp.where(place == self.pos, value, self.slots[at, k])
            self.slots[at, k] = value

    def start(self):
        for way in (0, 1):
            if self.split[way] > 0:
                self.fill(way, 0)
                self.copies[way][0].start()

    def forward(self, s):
        for way in (0, 1):
            if s < self.split[way]:
                copy = self.copies[way][s]
                if s + 1 < self.split[way]:
                    self.fill(way, s + 1, copy.wait_recv)
                    self.copies[way][s + 1].start()
                else:
                    copy.wait_recv()

    def entry(self, k):
        rights, lefts = self.split
        index, place = self.plan[0, rights][k]
        value = self.load(index)
        ahead = lax.rem(place - self.pos + self.n, self.n)
        if rights > 0:
            value = jnp.where(ahead > lefts, self.slots[rights, k], value)
        if lefts > 0:
            value = jnp.where((ahead > 0) & (ahead <= lefts), self.slots[rights + 1 + lefts, k], value)
        return value

    def finish(self):
        for way in (0, 1):
            for copy in self.copies[way]:
                copy.wait_send()


class Spread:
    def __init__(self, table, pos, n, peer_at, send, recv):
        order = sorted(range(1, n), key=lambda d: -min(d, n - d))
        self.copies = [remote(table.at[pos], table.at[pos], send.at[d - 1], recv.at[d - 1], peer_at(d)) for d in order]

    def start(self):
        for copy in self.copies:
            copy.start()

    steps = 1

    def forward(self, s):
        for copy in self.copies:
            copy.wait_recv()

    def finish(self):
        for copy in self.copies:
            copy.wait_send()


CHAINS = {8: ((-4, -3), (-2, -1), (2, 1), (3,)), 4: ((-2, -1), (1,)), 2: ((-1,),)}


class Relay:
    def __init__(self, table, lists, slots, pos, n, peer_at, send, recv, group_at, index_of, place_of):
        self.table, self.slots, self.pos, self.n = table, slots, pos, n
        self.chains = CHAINS[n]
        self.plan, self.first, self.second = {}, [], []
        count = lists.shape[0]
        targets = [0] + [-offset for chain in self.chains for offset in chain]
        for away in targets:
            group = group_at(lax.rem(pos + away + n, n))
            items = [lists[k, group] for k in range(count)]
            self.plan[away] = [(index_of(item), place_of(item)) for item in items]
        for c, chain in enumerate(self.chains):
            at = 3 * c
            if len(chain) == 1:
                self.first.append(remote(slots.at[at], slots.at[at + 2], send.at[c, 0], recv.at[c, 0], peer_at(-chain[0])))
                self.second.append(None)
            else:
                self.first.append(
                    remote(slots.at[at], slots.at[at + 1], send.at[c, 0], recv.at[c, 0], peer_at(chain[1] - chain[0]))
                )
                self.second.append(
                    remote(slots.at[at + 1], slots.at[at + 2], send.at[c, 1], recv.at[c, 1], peer_at(-chain[1]))
                )

    def start(self):
        for c, chain in enumerate(self.chains):
            for k, (index, _) in enumerate(self.plan[-chain[0]]):
                self.slots[3 * c, k] = self.table[index]
            self.first[c].start()

    steps = 2

    def forward(self, s):
        if s == 1:
            for c, chain in enumerate(self.chains):
                (self.first if len(chain) == 1 else self.second)[c].wait_recv()
            return
        for c, chain in enumerate(self.chains):
            if len(chain) == 2:
                plan = self.plan[-chain[1]]
                mine = [self.table[index] for index, _ in plan]
                self.first[c].wait_recv()
                for k, (_, place) in enumerate(plan):
                    self.slots[3 * c + 1, k] = jnp.where(place == self.pos, mine[k], self.slots[3 * c + 1, k])
                self.second[c].start()

    def entry(self, k):
        index, place = self.plan[0][k]
        value = self.table[index]
        ahead = lax.rem(place - self.pos + self.n, self.n)
        for c, chain in enumerate(self.chains):
            here = ahead == (chain[0] + self.n) % self.n
            if len(chain) == 2:
                here = here | (ahead == (chain[1] + self.n) % self.n)
            value = jnp.where(here, self.slots[3 * c + 2, k], value)
        return value

    def finish(self):
        for copy in self.first + [copy for copy in self.second if copy is not None]:
            copy.wait_send()


def remote(src, dst, send, recv, peer):
    return pltpu.make_async_remote_copy(
        src_ref=src, dst_ref=dst, send_sem=send, recv_sem=recv, device_id=peer, device_id_type=MESH
    )


PREV_PARTS = 4
DIRECT = "du"
SCHEDULE = (
    "D0", "U0", "K0", "V0", "p1", "D1", "U1", "K1", "V1", "p1", "D2", "U2",
    "K2", "V2", "p2", "D3", "U3", "d*", "u*", "K3", "V3", "d0", "u0", "p8",
    "k*", "v*", "P", "O", "k0", "v0", "R", "k1", "v1", "B", "B", "k2",
    "v2", "B", "B",
)
FACTOR = math.log2(math.e) * HEAD_WIDTH ** -0.5
NT = (((1,), (1,)), ((), ()))
TN = (((0,), (0,)), ((), ()))


def fused_kernel(
    ny, nz, ntp,
    page_list, adapter_list, page_entry_ref, adapter_entry_ref,
    ids_hbm, x_hbm, q_hbm, k_hbm, v_hbm, cache_hbm, down_hbm, up_hbm,
    out_hbm,
    down_tab, up_tab, kpage_tab, vpage_tab,
    down_slots, up_slots, kpage_slots, vpage_slots,
    x_ref, q_ref, ids_ref, idprev_ref, code_ref, down_all, up_all,
    keys, values, values_t, key_ids, kpages, vpages_t,
    parts, from_pair, half_sum, from_x, lowrank_ref,
    queries, tops, sums_ref, mixed_ref, out_ref,
    gather_send, gather_recv, relay_send, relay_recv, slot_send, slot_recv, prev_send, prev_recv, pair_send, pair_recv, x_send, x_recv,
    here, done,
):
    group = lax.axis_index("grp")
    tp = lax.axis_index("tp")
    groups = ny * nz
    y, z = lax.div(group, nz), lax.rem(group, nz)
    z_peers = ((y * nz + lax.rem(z + 1, nz), tp), (y * nz + lax.rem(z + nz - 1, nz), tp))
    y_peers = ((lax.rem(y + 1, ny) * nz + z, tp), (lax.rem(y + ny - 1, ny) * nz + z, tp))
    after = (lax.rem(group + 1, groups), tp)
    before = (lax.rem(group + groups - 1, groups), tp)
    core = lax.rem(tp, 2)
    pair = (group, tp + 1 - 2 * core)
    x_peers = [(group, lax.rem(tp + 2 * d, ntp)) for d in range(1, ntp // 2)]

    barrier = pltpu.get_barrier_semaphore()
    def z_at(offset):
        return (y * nz + lax.rem(z + offset + nz, nz), tp)

    def y_at(offset):
        return (lax.rem(y + offset + ny, ny) * nz + z, tp)

    greeted = [z_at(d) for d in range(1, nz)] + [y_at(d) for d in range(1, ny)] + [after, before, pair] + x_peers
    for peer in greeted:
        pl.semaphore_signal(barrier, inc=1, device_id=peer, device_id_type=MESH)

    stored, rank = down_hbm.shape[0], down_hbm.shape[1]
    tokens = k_hbm.shape[0]
    chunks = tokens // BLOCK
    listed, plisted = adapter_list.shape[0], page_list.shape[0]
    half = plisted // 2

    own = [
        pltpu.make_async_copy(down_hbm, down_tab.at[z], here.at[0]),
        pltpu.make_async_copy(up_hbm, up_tab.at[y], here.at[1]),
        pltpu.make_async_copy(cache_hbm.at[:, 0], kpage_tab.at[z], here.at[2]),
        pltpu.make_async_copy(cache_hbm.at[:, 1], vpage_tab.at[y], here.at[3]),
    ]
    own_rows = pl.ds(tokens, tokens)
    staged = [
        pltpu.make_async_copy(ids_hbm, ids_ref, here.at[4]),
        pltpu.make_async_copy(x_hbm, x_ref, here.at[5]),
        pltpu.make_async_copy(q_hbm, q_ref, here.at[6]),
        pltpu.make_async_copy(k_hbm, keys.at[own_rows], here.at[7]),
        pltpu.make_async_copy(v_hbm, values.at[own_rows], here.at[8]),
    ]
    for copy in own + staged:
        copy.start()

    zs, ys = ring_split(nz, False), ring_split(ny, True)
    by_y = (lambda target: target * nz + z, lambda item: (lax.rem(lax.div(item, stored), nz), lax.rem(item, stored)),
            lambda item: lax.div(item, stored * nz))
    by_z = (lambda target: y * nz + target, lambda item: (lax.div(item, stored * nz), lax.rem(item, stored)),
            lambda item: lax.rem(lax.div(item, stored), nz))

    def gather_z(direct, table, at):
        if direct:
            return Spread(table, z, nz, z_at, gather_send.at[at], gather_recv.at[at])
        return Gather(table, z, nz, z_peers, zs, gather_send.at[at], gather_recv.at[at])

    def gather_y(direct, table, at):
        if direct:
            return Spread(table, y, ny, y_at, gather_send.at[at], gather_recv.at[at])
        return Gather(table, y, ny, y_peers, ys, gather_send.at[at], gather_recv.at[at])

    def slots_y(relay, table, lists, picks, slots, at):
        if relay:
            return Relay(table, lists, slots, y, ny, y_at, relay_send.at[at], relay_recv.at[at], *by_y)
        ring = Slots(
            lambda index: table[index], lists, picks, slots, y, ny, y_peers, ys, slot_send.at[at], slot_recv.at[at], *by_y
        )
        ring.prepare()
        return ring

    def slots_z(relay, table, lists, picks, slots, at):
        if relay:
            return Relay(table, lists, slots, z, nz, z_at, relay_send.at[at], relay_recv.at[at], *by_z)
        ring = Slots(
            lambda index: table[index], lists, picks, slots, z, nz, z_peers, zs, slot_send.at[at], slot_recv.at[at], *by_z
        )
        ring.prepare()
        return ring

    flows = {
        "D": [gather_z("D" in DIRECT, down_tab, 0)],
        "U": [gather_y("U" in DIRECT, up_tab, 1)],
        "K": [gather_z("K" in DIRECT, kpage_tab, 2)],
        "V": [gather_y("V" in DIRECT, vpage_tab, 3)],
    }
    every = range(listed)

    def make_slots():
        flows["d"] = [slots_y("d" in DIRECT, down_tab, adapter_list, every, down_slots, 0)]
        flows["u"] = [slots_z("u" in DIRECT, up_tab, adapter_list, every, up_slots, 1)]
        flows["k"], flows["v"] = [], []
        for part in range(2):
            picks = range(part * half, part * half + half)
            flows["k"].append(slots_y(False, kpage_tab, page_list, picks, kpage_slots.at[part], 2 + part))
            flows["v"].append(slots_z(False, vpage_tab, page_list, picks, vpage_slots.at[part], 4 + part))

    state = {name: 0 for name in "DUKVduvk"}

    def advance(name, upto=None):
        steps = max(flow.steps for flow in flows[name])
        while state[name] < (steps if upto is None else min(upto, steps)):
            for flow in flows[name]:
                if state[name] < flow.steps:
                    flow.forward(state[name])
            state[name] += 1

    rows = tokens // PREV_PARTS
    prevs = []
    for part in range(PREV_PARTS):
        at = pl.ds(part * rows, rows)
        prevs.append(remote(k_hbm.at[at], keys.at[at], prev_send.at[0, part], prev_recv.at[0, part], after))
        prevs.append(remote(v_hbm.at[at], values.at[at], prev_send.at[1, part], prev_recv.at[1, part], after))
    idprev = remote(ids_hbm, idprev_ref, prev_send.at[2, 0], prev_recv.at[2, 0], after)
    waiting = list(prevs)

    def some_prev(count):
        for _ in range(min(count, len(waiting))):
            waiting.pop(0).start()

    pl.semaphore_wait(barrier, len(greeted))
    for copy, name in zip(own, "DUKV"):
        copy.wait()
        flows[name][0].start()
    idprev.start()
    make_slots()
    staged[0].wait()
    code_columns = as_columns(page_entry_ref[...] * listed + adapter_entry_ref[...])
    for c in range(chunks):
        code_ref[pl.ds(c, 1), :] = token_codes(ids_ref[pl.ds(c, 1), :], code_columns)
        key_ids[pl.ds(tokens + c * BLOCK, BLOCK), :] = as_columns(ids_ref[pl.ds(c, 1), :])

    each = chunks // 2
    mine = pl.ds(core * each, each)
    theirs = pl.ds((1 - core) * each, each)
    to_pair = remote(parts.at[theirs], from_pair, pair_send.at[0], pair_recv.at[0], pair)
    to_x = [
        remote(half_sum, from_x.at[d], x_send.at[d], x_recv.at[d], peer) for d, peer in enumerate(x_peers)
    ]
    back = remote(lowrank_ref.at[mine], lowrank_ref.at[mine], pair_send.at[1], pair_recv.at[1], pair)

    def project():
        advance("d")
        for k in range(listed):
            down_all[k * rank:(k + 1) * rank, :] = flows["d"][0].entry(k)
        staged[1].wait()
        partial = lax.dot_general(down_all[...], x_ref[...], NT, preferred_element_type=F32)
        for c in range(chunks):
            entry = lax.rem(code_ref[pl.ds(c, 1), :], listed)
            total = jnp.zeros((rank, BLOCK), F32)
            for k in range(listed):
                total = jnp.where(entry == k, partial[k * rank:(k + 1) * rank, c * BLOCK:(c + 1) * BLOCK], total)
            parts[c] = total
        to_pair.start()
        to_pair.wait_recv()
        half_sum[...] = parts[mine] + from_pair[...]
        for copy in to_x:
            copy.start()

    def own_values():
        for copy in staged[2:]:
            copy.wait()
        for c in range(chunks):
            at = tokens + c * BLOCK
            values_t[:, at:at + BLOCK] = values[at:at + BLOCK, :].T

    def ready():
        for copy in prevs + [idprev]:
            copy.wait_recv()
        first = group == 0
        for c in range(chunks):
            at = c * BLOCK
            values_t[:, at:at + BLOCK] = values[at:at + BLOCK, :].T
            key_ids[at:at + BLOCK, :] = as_columns(jnp.where(first, -1, idprev_ref[pl.ds(c, 1), :]))
        advance("u")
        for k in range(listed):
            up_all[k * rank:(k + 1) * rank, :] = flows["u"][0].entry(k)
        total = half_sum[...]
        for d, copy in enumerate(to_x):
            copy.wait_recv()
            total = total + from_x[d]
        lowrank_ref[mine] = total.astype(BF16)
        back.start()
        back.wait_recv()

    band = tokens + BLOCK
    later = lax.broadcasted_iota(jnp.int32, (BLOCK, BLOCK), 0)
    sooner = lax.broadcasted_iota(jnp.int32, (BLOCK, BLOCK), 1)
    causal = later <= sooner

    def band_block(i, carry):
        start = pl.multiple_of(i * BLOCK, BLOCK)
        entry = lax.rem(code_ref[pl.ds(i, 1), :], listed)
        low = lowrank_ref[i]
        wide = jnp.concatenate([jnp.where(entry == k, low, jnp.zeros_like(low)) for k in range(listed)], axis=0)
        update = lax.dot_general(wide, up_all[...], TN, preferred_element_type=F32)
        query = (q_ref[pl.ds(start, BLOCK), :].astype(F32) + ADAPTER_SCALE * update).astype(BF16)
        stacked = jnp.concatenate([query[:, h * HEAD_WIDTH:(h + 1) * HEAD_WIDTH] for h in range(PER_KV)], axis=0)
        queries[i] = stacked
        scores = lax.dot_general(keys[pl.ds(start, band), :], stacked, NT, preferred_element_type=F32)
        ids_row = ids_ref[pl.ds(i, 1), :]
        masks = [key_ids[pl.ds(start + c * BLOCK, BLOCK), :] == ids_row for c in range(chunks + 1)]
        masks[chunks] = masks[chunks] & causal
        weights = []
        for h in range(PER_KV):
            across = slice(h * BLOCK, (h + 1) * BLOCK)
            pieces = [
                jnp.where(masks[c], scores[c * BLOCK:(c + 1) * BLOCK, across], F32(-1e30)) for c in range(chunks + 1)
            ]
            top = jnp.max(functools.reduce(jnp.maximum, pieces), axis=0, keepdims=True)
            expos = [jnp.exp2((piece - top) * FACTOR) for piece in pieces]
            tops[i, h:h + 1, :] = top
            sums_ref[i, h:h + 1, :] = jnp.sum(functools.reduce(jnp.add, expos), axis=0, keepdims=True)
            weights.append(jnp.concatenate([e.astype(BF16) for e in expos], axis=0))
        mixed_ref[i] = jnp.dot(
            values_t[:, pl.ds(start, band)], jnp.concatenate(weights, axis=1), preferred_element_type=F32
        )
        return carry

    quarter = max(chunks // 4, 1)
    turn = 0
    for token in SCHEDULE:
        name, what = token[0], token[1:]
        if name in state:
            if what == "*":
                advance(name.upper())
                for flow in flows[name]:
                    flow.start()
            else:
                advance(name, int(what) + 1)
        elif name == "p":
            some_prev(int(what))
        elif name == "P":
            project()
        elif name == "O":
            own_values()
        elif name == "R":
            some_prev(len(waiting))
            ready()
        elif name == "B" and turn * quarter < chunks:
            lax.fori_loop(turn * quarter, turn * quarter + quarter, band_block, 0, unroll=quarter)
            turn += 1
    advance("k")
    advance("v")

    for part in range(2):
        for k in range(half):
            at = (part * half + k) * PAGE
            kpages[at:at + PAGE, :] = flows["k"][part].entry(k)
            vpages_t[:, at:at + PAGE] = flows["v"][part].entry(k).T

    def page_block(i, carry):
        start = pl.multiple_of(i * BLOCK, BLOCK)
        scores = lax.dot_general(kpages[...], queries[i], NT, preferred_element_type=F32)
        page_of = lax.div(code_ref[pl.ds(i, 1), :], listed)
        weights, scales = [], []
        for h in range(PER_KV):
            across = slice(h * BLOCK, (h + 1) * BLOCK)
            piece = scores[:PAGE, across]
            for k in range(1, plisted):
                piece = jnp.where(page_of == k, scores[k * PAGE:(k + 1) * PAGE, across], piece)
            before_top = tops[i, h:h + 1, :]
            top = jnp.maximum(jnp.max(piece, axis=0, keepdims=True), before_top)
            expo = jnp.exp2((piece - top) * FACTOR)
            shrink = jnp.exp2((before_top - top) * FACTOR)
            total = sums_ref[i, h:h + 1, :] * shrink + jnp.sum(expo, axis=0, keepdims=True)
            scales.append((shrink, 1.0 / total))
            weights.append(
                jnp.concatenate([jnp.where(page_of == k, expo, 0.0).astype(BF16) for k in range(plisted)], axis=0)
            )
        mixed = jnp.dot(vpages_t[...], jnp.concatenate(weights, axis=1), preferred_element_type=F32)
        for h in range(PER_KV):
            across = slice(h * BLOCK, (h + 1) * BLOCK)
            shrink, inverse = scales[h]
            value = (mixed_ref[i, :, across] * shrink + mixed[:, across]) * inverse
            out_ref[pl.ds(start, BLOCK), h * HEAD_WIDTH:(h + 1) * HEAD_WIDTH] = value.T.astype(BF16)
        at = pl.ds(start, BLOCK)
        pltpu.make_async_copy(out_ref.at[at], out_hbm.at[at], done.at[i]).start()
        return carry

    lax.fori_loop(0, chunks, page_block, 0, unroll=2)

    for copy in prevs + [idprev, to_pair, back] + to_x:
        copy.wait_send()
    for some in flows.values():
        for flow in some:
            flow.finish()
    for i in range(chunks):
        at = pl.ds(i * BLOCK, BLOCK)
        pltpu.make_async_copy(out_ref.at[at], out_hbm.at[at], done.at[i]).wait()


def fused(ny, nz, ntp, page_list, adapter_list, page_entry, adapter_entry, ids, x, q, k, v, cache, down, up):
    chunks = ids.shape[0]
    tokens = k.shape[0]
    stored, rank, features = down.shape
    listed, plisted = adapter_list.shape[0], page_list.shape[0]
    half = plisted // 2
    vmem = pl.BlockSpec(memory_space=pltpu.VMEM)
    smem = pl.BlockSpec(memory_space=pltpu.SMEM)
    hbm = pl.BlockSpec(memory_space=pltpu.HBM)
    most = max(ny, nz) - 1
    nx = max(ntp // 2 - 1, 1)
    dma = pltpu.SemaphoreType.DMA
    stack = PER_KV * BLOCK
    return pl.pallas_call(
        functools.partial(fused_kernel, ny, nz, ntp),
        out_shape=jax.ShapeDtypeStruct(q.shape, BF16),
        in_specs=[smem, smem, vmem, vmem] + [hbm] * 8,
        out_specs=hbm,
        scratch_shapes=[
            pltpu.VMEM((nz, stored, rank, features), BF16),
            pltpu.VMEM((ny, stored, rank, features), BF16),
            pltpu.VMEM((nz, stored, PAGE, HEAD_WIDTH), BF16),
            pltpu.VMEM((ny, stored, PAGE, HEAD_WIDTH), BF16),
            pltpu.VMEM((max(3 * len(CHAINS[ny]), ny + 1), listed, rank, features), BF16),
            pltpu.VMEM((max(3 * len(CHAINS[nz]), nz + 1), listed, rank, features), BF16),
            pltpu.VMEM((2, ny + 1, half, PAGE, HEAD_WIDTH), BF16),
            pltpu.VMEM((2, nz + 1, half, PAGE, HEAD_WIDTH), BF16),
            pltpu.VMEM(x.shape, BF16),
            pltpu.VMEM(q.shape, BF16),
            pltpu.VMEM(ids.shape, jnp.int32),
            pltpu.VMEM(ids.shape, jnp.int32),
            pltpu.VMEM(ids.shape, jnp.int32),
            pltpu.VMEM((listed * rank, features), BF16),
            pltpu.VMEM((listed * rank, features), BF16),
            pltpu.VMEM((2 * tokens, HEAD_WIDTH), BF16),
            pltpu.VMEM((2 * tokens, HEAD_WIDTH), BF16),
            pltpu.VMEM((HEAD_WIDTH, 2 * tokens), BF16),
            pltpu.VMEM((2 * tokens, BLOCK), jnp.int32),
            pltpu.VMEM((plisted * PAGE, HEAD_WIDTH), BF16),
            pltpu.VMEM((HEAD_WIDTH, plisted * PAGE), BF16),
            pltpu.VMEM((chunks, rank, BLOCK), F32),
            pltpu.VMEM((chunks // 2, rank, BLOCK), F32),
            pltpu.VMEM((chunks // 2, rank, BLOCK), F32),
            pltpu.VMEM((nx, chunks // 2, rank, BLOCK), F32),
            pltpu.VMEM((chunks, rank, BLOCK), BF16),
            pltpu.VMEM((chunks, stack, HEAD_WIDTH), BF16),
            pltpu.VMEM((chunks, 8, BLOCK), F32),
            pltpu.VMEM((chunks, 8, BLOCK), F32),
            pltpu.VMEM((chunks, HEAD_WIDTH, stack), F32),
            pltpu.VMEM(q.shape, BF16),
            dma((4, most)), dma((4, most)), dma((2, 4, 2)), dma((2, 4, 2)), dma((6, most)), dma((6, most)),
            dma((3, PREV_PARTS)), dma((3, PREV_PARTS)),
            dma((2,)), dma((2,)), dma((nx,)), dma((nx,)),
            dma((9,)), dma((chunks,)),
        ],
        compiler_params=pltpu.CompilerParams(
            collective_id=0, has_side_effects=True, vmem_limit_bytes=56 * 1024 * 1024
        ),
        name="fused",
    )(page_list, adapter_list, page_entry, adapter_entry, ids, x, q, k, v, cache, down, up)


def solution(mesh, nz=8):
    groups, ntp = mesh.shape["grp"], mesh.shape["tp"]
    ny = groups // nz

    def local(x, q, k, v, request, cache, down, up, page_list, adapter_list, page_entry, adapter_entry):
        return fused(
            ny, nz, ntp, page_list.T, adapter_list.T, page_entry.reshape(1, -1), adapter_entry.reshape(1, -1),
            request.reshape(-1, BLOCK), x, q, k, v, cache, down, up,
        )

    placed = (
        P("grp", "tp"),
        P("grp", "tp"),
        P("grp", "tp"),
        P("grp", "tp"),
        P("grp"),
        P("grp", None, None, "tp"),
        P("grp", None, "tp"),
        P("grp", None, "tp"),
        P(),
        P(),
        P(),
        P(),
    )
    return jax.shard_map(local, mesh=mesh, in_specs=placed, out_specs=P("grp", "tp"), check_vma=False)
```

```python
import functools
import math

import jax
import jax.numpy as jnp
from jax import lax
from jax.experimental import pallas as pl
from jax.experimental.pallas import tpu as pltpu
from jax.sharding import PartitionSpec as P

PER_KV = 4
HEAD_WIDTH = 128
PAGE = 128
BLOCK = 128
ADAPTER_SCALE = 0.5
MESH = pl.DeviceIdType.MESH
F32 = jnp.float32
BF16 = jnp.bfloat16


def ring_split(n, heavy_right):
    more, fewer = n // 2, (n - 1) // 2
    return (more, fewer) if heavy_right else (fewer, more)


def token_codes(ids_row, table_columns):
    requests = table_columns.shape[0]
    numbers = lax.broadcasted_iota(jnp.int32, (requests, ids_row.shape[1]), 0)
    return jnp.sum(jnp.where(numbers == ids_row, table_columns, 0), axis=0, keepdims=True)


def as_columns(row):
    return jnp.broadcast_to(row, (128, row.shape[1])).T


class Gather:
    def __init__(self, table, pos, n, peers, split, send, recv):
        self.copies = []
        for s in range(1, max(split) + 1):
            now = []
            for way in (0, 1):
                if s <= split[way]:
                    origin = lax.rem(pos - (s - 1) + n, n) if way == 0 else lax.rem(pos + (s - 1), n)
                    at = s - 1 if way == 0 else split[0] + s - 1
                    now.append(remote(table.at[origin], table.at[origin], send.at[at], recv.at[at], peers[way]))
                else:
                    now.append(None)
            self.copies.append(now)
        self.steps = len(self.copies)

    def start(self):
        for copy in self.copies[0]:
            if copy is not None:
                copy.start()

    def forward(self, s):
        for way, copy in enumerate(self.copies[s]):
            if copy is not None:
                copy.wait_recv()
                if s + 1 < self.steps and self.copies[s + 1][way] is not None:
                    self.copies[s + 1][way].start()

    def finish(self):
        for now in self.copies:
            for copy in now:
                if copy is not None:
                    copy.wait_send()


class Slots:
    def __init__(self, load, lists, picks, slots, pos, n, peers, split, send, recv, group_at, index_of, place_of):
        self.load, self.lists, self.picks, self.slots, self.pos, self.n = load, lists, picks, slots, pos, n
        self.split = split
        self.base = (0, split[0] + 1)
        self.group_at, self.index_of, self.place_of = group_at, index_of, place_of
        self.copies = []
        for way in (0, 1):
            base = self.base[way]
            sems = 0 if way == 0 else split[0]
            self.copies.append(
                [
                    remote(slots.at[base + s], slots.at[base + s + 1], send.at[sems + s], recv.at[sems + s], peers[way])
                    for s in range(split[way])
                ]
            )
        self.steps = max(split)
        self.plan = {}

    def prepare(self):
        for way in (0, 1):
            for s in range(self.split[way] + 1):
                away = self.split[way] - s
                target = lax.rem(self.pos + away, self.n) if way == 0 else lax.rem(self.pos - away + self.n, self.n)
                group = self.group_at(target)
                items = [self.lists[k, group] for k in self.picks]
                self.plan[way, s] = [(self.index_of(item), self.place_of(item)) for item in items]

    def fill(self, way, s, wait=None):
        plan = self.plan[way, s]
        mine = [self.load(index) for index, _ in plan]
        if wait is not None:
            wait()
        at = self.base[way] + s
        for k, (_, place) in enumerate(plan):
            value = mine[k]
            if s > 0:
                value = jnp.where(place == self.pos, value, self.slots[at, k])
            self.slots[at, k] = value

    def start(self):
        for way in (0, 1):
            if self.split[way] > 0:
                self.fill(way, 0)
                self.copies[way][0].start()

    def forward(self, s):
        for way in (0, 1):
            if s < self.split[way]:
                copy = self.copies[way][s]
                if s + 1 < self.split[way]:
                    self.fill(way, s + 1, copy.wait_recv)
                    self.copies[way][s + 1].start()
                else:
                    copy.wait_recv()

    def entry(self, k):
        rights, lefts = self.split
        index, place = self.plan[0, rights][k]
        value = self.load(index)
        ahead = lax.rem(place - self.pos + self.n, self.n)
        if rights > 0:
            value = jnp.where(ahead > lefts, self.slots[rights, k], value)
        if lefts > 0:
            value = jnp.where((ahead > 0) & (ahead <= lefts), self.slots[rights + 1 + lefts, k], value)
        return value

    def finish(self):
        for way in (0, 1):
            for copy in self.copies[way]:
                copy.wait_send()


class Spread:
    def __init__(self, table, pos, n, peer_at, send, recv):
        order = sorted(range(1, n), key=lambda d: -min(d, n - d))
        self.copies = [remote(table.at[pos], table.at[pos], send.at[d - 1], recv.at[d - 1], peer_at(d)) for d in order]

    def start(self):
        for copy in self.copies:
            copy.start()

    steps = 1

    def forward(self, s):
        for copy in self.copies:
            copy.wait_recv()

    def finish(self):
        for copy in self.copies:
            copy.wait_send()


CHAINS = {8: ((-4, -3), (-2, -1), (2, 1), (3,)), 4: ((-2, -1), (1,)), 2: ((-1,),)}


class Relay:
    def __init__(self, table, lists, slots, pos, n, peer_at, send, recv, group_at, index_of, place_of):
        self.table, self.slots, self.pos, self.n = table, slots, pos, n
        self.chains = CHAINS[n]
        self.plan, self.first, self.second = {}, [], []
        count = lists.shape[0]
        targets = [0] + [-offset for chain in self.chains for offset in chain]
        for away in targets:
            group = group_at(lax.rem(pos + away + n, n))
            items = [lists[k, group] for k in range(count)]
            self.plan[away] = [(index_of(item), place_of(item)) for item in items]
        for c, chain in enumerate(self.chains):
            at = 3 * c
            if len(chain) == 1:
                self.first.append(remote(slots.at[at], slots.at[at + 2], send.at[c, 0], recv.at[c, 0], peer_at(-chain[0])))
                self.second.append(None)
            else:
                self.first.append(
                    remote(slots.at[at], slots.at[at + 1], send.at[c, 0], recv.at[c, 0], peer_at(chain[1] - chain[0]))
                )
                self.second.append(
                    remote(slots.at[at + 1], slots.at[at + 2], send.at[c, 1], recv.at[c, 1], peer_at(-chain[1]))
                )

    def start(self):
        for c, chain in enumerate(self.chains):
            for k, (index, _) in enumerate(self.plan[-chain[0]]):
                self.slots[3 * c, k] = self.table[index]
            self.first[c].start()

    steps = 2

    def forward(self, s):
        if s == 1:
            for c, chain in enumerate(self.chains):
                (self.first if len(chain) == 1 else self.second)[c].wait_recv()
            return
        for c, chain in enumerate(self.chains):
            if len(chain) == 2:
                plan = self.plan[-chain[1]]
                mine = [self.table[index] for index, _ in plan]
                self.first[c].wait_recv()
                for k, (_, place) in enumerate(plan):
                    self.slots[3 * c + 1, k] = jnp.where(place == self.pos, mine[k], self.slots[3 * c + 1, k])
                self.second[c].start()

    def entry(self, k):
        index, place = self.plan[0][k]
        value = self.table[index]
        ahead = lax.rem(place - self.pos + self.n, self.n)
        for c, chain in enumerate(self.chains):
            here = ahead == (chain[0] + self.n) % self.n
            if len(chain) == 2:
                here = here | (ahead == (chain[1] + self.n) % self.n)
            value = jnp.where(here, self.slots[3 * c + 2, k], value)
        return value

    def finish(self):
        for copy in self.first + [copy for copy in self.second if copy is not None]:
            copy.wait_send()


def remote(src, dst, send, recv, peer):
    return pltpu.make_async_remote_copy(
        src_ref=src, dst_ref=dst, send_sem=send, recv_sem=recv, device_id=peer, device_id_type=MESH
    )


PREV_PARTS = 4
PAGE_UNROLL = 4
DIRECT = "du"
SCHEDULE = (
    "D0", "U0", "K0", "V0", "p1", "D1", "U1", "K1", "V1", "p1", "D2", "U2",
    "K2", "V2", "p2", "D3", "U3", "d*", "u*", "K3", "V3", "d0", "u0", "p8",
    "k*", "v*", "P", "O", "k0", "v0", "R", "k1", "v1", "B", "B", "k2",
    "v2", "B", "B",
)
FACTOR = math.log2(math.e) * HEAD_WIDTH ** -0.5
NT = (((1,), (1,)), ((), ()))
TN = (((0,), (0,)), ((), ()))


def fused_kernel(
    ny, nz, ntp,
    page_list, adapter_list, page_entry_ref, adapter_entry_ref,
    ids_hbm, x_hbm, q_hbm, k_hbm, v_hbm, cache_hbm, down_hbm, up_hbm,
    out_hbm,
    down_tab, up_tab, kpage_tab, vpage_tab,
    down_slots, up_slots, kpage_slots, vpage_slots,
    x_ref, q_ref, ids_ref, idprev_ref, code_ref, down_all, up_all,
    keys, values, values_t, key_ids, kpages, vpages_t,
    parts, from_pair, half_sum, from_x, lowrank_ref,
    queries, tops, sums_ref, mixed_ref, out_ref,
    gather_send, gather_recv, relay_send, relay_recv, slot_send, slot_recv, prev_send, prev_recv, pair_send, pair_recv, x_send, x_recv,
    here, done,
):
    group = lax.axis_index("grp")
    tp = lax.axis_index("tp")
    groups = ny * nz
    y, z = lax.div(group, nz), lax.rem(group, nz)
    z_peers = ((y * nz + lax.rem(z + 1, nz), tp), (y * nz + lax.rem(z + nz - 1, nz), tp))
    y_peers = ((lax.rem(y + 1, ny) * nz + z, tp), (lax.rem(y + ny - 1, ny) * nz + z, tp))
    after = (lax.rem(group + 1, groups), tp)
    before = (lax.rem(group + groups - 1, groups), tp)
    core = lax.rem(tp, 2)
    pair = (group, tp + 1 - 2 * core)
    x_peers = [(group, lax.rem(tp + 2 * d, ntp)) for d in range(1, ntp // 2)]

    barrier = pltpu.get_barrier_semaphore()
    def z_at(offset):
        return (y * nz + lax.rem(z + offset + nz, nz), tp)

    def y_at(offset):
        return (lax.rem(y + offset + ny, ny) * nz + z, tp)

    greeted = [z_at(d) for d in range(1, nz)] + [y_at(d) for d in range(1, ny)] + [after, before, pair] + x_peers
    for peer in greeted:
        pl.semaphore_signal(barrier, inc=1, device_id=peer, device_id_type=MESH)

    stored, rank = down_hbm.shape[0], down_hbm.shape[1]
    tokens = k_hbm.shape[0]
    chunks = tokens // BLOCK
    listed, plisted = adapter_list.shape[0], page_list.shape[0]
    half = plisted // 2

    own = [
        pltpu.make_async_copy(down_hbm, down_tab.at[z], here.at[0]),
        pltpu.make_async_copy(up_hbm, up_tab.at[y], here.at[1]),
        pltpu.make_async_copy(cache_hbm.at[:, 0], kpage_tab.at[z], here.at[2]),
        pltpu.make_async_copy(cache_hbm.at[:, 1], vpage_tab.at[y], here.at[3]),
    ]
    own_rows = pl.ds(tokens, tokens)
    staged = [
        pltpu.make_async_copy(ids_hbm, ids_ref, here.at[4]),
        pltpu.make_async_copy(x_hbm, x_ref, here.at[5]),
        pltpu.make_async_copy(q_hbm, q_ref, here.at[6]),
        pltpu.make_async_copy(k_hbm, keys.at[own_rows], here.at[7]),
        pltpu.make_async_copy(v_hbm, values.at[own_rows], here.at[8]),
    ]
    for copy in own + staged:
        copy.start()

    zs, ys = ring_split(nz, False), ring_split(ny, True)
    by_y = (lambda target: target * nz + z, lambda item: (lax.rem(lax.div(item, stored), nz), lax.rem(item, stored)),
            lambda item: lax.div(item, stored * nz))
    by_z = (lambda target: y * nz + target, lambda item: (lax.div(item, stored * nz), lax.rem(item, stored)),
            lambda item: lax.rem(lax.div(item, stored), nz))

    def gather_z(direct, table, at):
        if direct:
            return Spread(table, z, nz, z_at, gather_send.at[at], gather_recv.at[at])
        return Gather(table, z, nz, z_peers, zs, gather_send.at[at], gather_recv.at[at])

    def gather_y(direct, table, at):
        if direct:
            return Spread(table, y, ny, y_at, gather_send.at[at], gather_recv.at[at])
        return Gather(table, y, ny, y_peers, ys, gather_send.at[at], gather_recv.at[at])

    def slots_y(relay, table, lists, picks, slots, at):
        if relay:
            return Relay(table, lists, slots, y, ny, y_at, relay_send.at[at], relay_recv.at[at], *by_y)
        ring = Slots(
            lambda index: table[index], lists, picks, slots, y, ny, y_peers, ys, slot_send.at[at], slot_recv.at[at], *by_y
        )
        ring.prepare()
        return ring

    def slots_z(relay, table, lists, picks, slots, at):
        if relay:
            return Relay(table, lists, slots, z, nz, z_at, relay_send.at[at], relay_recv.at[at], *by_z)
        ring = Slots(
            lambda index: table[index], lists, picks, slots, z, nz, z_peers, zs, slot_send.at[at], slot_recv.at[at], *by_z
        )
        ring.prepare()
        return ring

    flows = {
        "D": [gather_z("D" in DIRECT, down_tab, 0)],
        "U": [gather_y("U" in DIRECT, up_tab, 1)],
        "K": [gather_z("K" in DIRECT, kpage_tab, 2)],
        "V": [gather_y("V" in DIRECT, vpage_tab, 3)],
    }
    every = range(listed)

    def make_slots():
        flows["d"] = [slots_y("d" in DIRECT, down_tab, adapter_list, every, down_slots, 0)]
        flows["u"] = [slots_z("u" in DIRECT, up_tab, adapter_list, every, up_slots, 1)]
        flows["k"], flows["v"] = [], []
        for part in range(2):
            picks = range(part * half, part * half + half)
            flows["k"].append(slots_y(False, kpage_tab, page_list, picks, kpage_slots.at[part], 2 + part))
            flows["v"].append(slots_z(False, vpage_tab, page_list, picks, vpage_slots.at[part], 4 + part))

    state = {name: 0 for name in "DUKVduvk"}

    def advance(name, upto=None):
        steps = max(flow.steps for flow in flows[name])
        while state[name] < (steps if upto is None else min(upto, steps)):
            for flow in flows[name]:
                if state[name] < flow.steps:
                    flow.forward(state[name])
            state[name] += 1

    rows = tokens // PREV_PARTS
    prevs = []
    for part in range(PREV_PARTS):
        at = pl.ds(part * rows, rows)
        prevs.append(remote(k_hbm.at[at], keys.at[at], prev_send.at[0, part], prev_recv.at[0, part], after))
        prevs.append(remote(v_hbm.at[at], values.at[at], prev_send.at[1, part], prev_recv.at[1, part], after))
    idprev = remote(ids_hbm, idprev_ref, prev_send.at[2, 0], prev_recv.at[2, 0], after)
    waiting = list(prevs)

    def some_prev(count):
        for _ in range(min(count, len(waiting))):
            waiting.pop(0).start()

    pl.semaphore_wait(barrier, len(greeted))
    for copy, name in zip(own, "DUKV"):
        copy.wait()
        flows[name][0].start()
    idprev.start()
    make_slots()
    staged[0].wait()
    code_columns = as_columns(page_entry_ref[...] * listed + adapter_entry_ref[...])
    for c in range(chunks):
        code_ref[pl.ds(c, 1), :] = token_codes(ids_ref[pl.ds(c, 1), :], code_columns)
        key_ids[pl.ds(tokens + c * BLOCK, BLOCK), :] = as_columns(ids_ref[pl.ds(c, 1), :])

    each = chunks // 2
    mine = pl.ds(core * each, each)
    theirs = pl.ds((1 - core) * each, each)
    to_pair = remote(parts.at[theirs], from_pair, pair_send.at[0], pair_recv.at[0], pair)
    to_x = [
        remote(half_sum, from_x.at[d], x_send.at[d], x_recv.at[d], peer) for d, peer in enumerate(x_peers)
    ]
    back = remote(lowrank_ref.at[mine], lowrank_ref.at[mine], pair_send.at[1], pair_recv.at[1], pair)

    def project():
        advance("d")
        for k in range(listed):
            down_all[k * rank:(k + 1) * rank, :] = flows["d"][0].entry(k)
        staged[1].wait()
        partial = lax.dot_general(down_all[...], x_ref[...], NT, preferred_element_type=F32)
        for c in range(chunks):
            entry = lax.rem(code_ref[pl.ds(c, 1), :], listed)
            total = jnp.zeros((rank, BLOCK), F32)
            for k in range(listed):
                total = jnp.where(entry == k, partial[k * rank:(k + 1) * rank, c * BLOCK:(c + 1) * BLOCK], total)
            parts[c] = total
        to_pair.start()
        to_pair.wait_recv()
        half_sum[...] = parts[mine] + from_pair[...]
        for copy in to_x:
            copy.start()

    def own_values():
        for copy in staged[2:]:
            copy.wait()
        for c in range(chunks):
            at = tokens + c * BLOCK
            values_t[:, at:at + BLOCK] = values[at:at + BLOCK, :].T

    def ready():
        for copy in prevs + [idprev]:
            copy.wait_recv()
        first = group == 0
        for c in range(chunks):
            at = c * BLOCK
            values_t[:, at:at + BLOCK] = values[at:at + BLOCK, :].T
            key_ids[at:at + BLOCK, :] = as_columns(jnp.where(first, -1, idprev_ref[pl.ds(c, 1), :]))
        advance("u")
        for k in range(listed):
            up_all[k * rank:(k + 1) * rank, :] = flows["u"][0].entry(k)
        total = half_sum[...]
        for d, copy in enumerate(to_x):
            copy.wait_recv()
            total = total + from_x[d]
        lowrank_ref[mine] = total.astype(BF16)
        back.start()
        back.wait_recv()

    band = tokens + BLOCK
    later = lax.broadcasted_iota(jnp.int32, (BLOCK, BLOCK), 0)
    sooner = lax.broadcasted_iota(jnp.int32, (BLOCK, BLOCK), 1)
    causal = later <= sooner

    def band_block(i, carry):
        start = pl.multiple_of(i * BLOCK, BLOCK)
        entry = lax.rem(code_ref[pl.ds(i, 1), :], listed)
        low = lowrank_ref[i]
        wide = jnp.concatenate([jnp.where(entry == k, low, jnp.zeros_like(low)) for k in range(listed)], axis=0)
        update = lax.dot_general(wide, up_all[...], TN, preferred_element_type=F32)
        query = (q_ref[pl.ds(start, BLOCK), :].astype(F32) + ADAPTER_SCALE * update).astype(BF16)
        stacked = jnp.concatenate([query[:, h * HEAD_WIDTH:(h + 1) * HEAD_WIDTH] for h in range(PER_KV)], axis=0)
        queries[i] = stacked
        scores = lax.dot_general(keys[pl.ds(start, band), :], stacked, NT, preferred_element_type=F32)
        ids_row = ids_ref[pl.ds(i, 1), :]
        masks = [key_ids[pl.ds(start + c * BLOCK, BLOCK), :] == ids_row for c in range(chunks + 1)]
        masks[chunks] = masks[chunks] & causal
        weights = []
        for h in range(PER_KV):
            across = slice(h * BLOCK, (h + 1) * BLOCK)
            pieces = [
                jnp.where(masks[c], scores[c * BLOCK:(c + 1) * BLOCK, across], F32(-1e30)) for c in range(chunks + 1)
            ]
            top = jnp.max(functools.reduce(jnp.maximum, pieces), axis=0, keepdims=True)
            expos = [jnp.exp2((piece - top) * FACTOR) for piece in pieces]
            tops[i, h:h + 1, :] = top
            sums_ref[i, h:h + 1, :] = jnp.sum(functools.reduce(jnp.add, expos), axis=0, keepdims=True)
            weights.append(jnp.concatenate([e.astype(BF16) for e in expos], axis=0))
        mixed_ref[i] = jnp.dot(
            values_t[:, pl.ds(start, band)], jnp.concatenate(weights, axis=1), preferred_element_type=F32
        )
        return carry

    quarter = max(chunks // 4, 1)
    turn = 0
    for token in SCHEDULE:
        name, what = token[0], token[1:]
        if name in state:
            if what == "*":
                advance(name.upper())
                for flow in flows[name]:
                    flow.start()
            else:
                advance(name, int(what) + 1)
        elif name == "p":
            some_prev(int(what))
        elif name == "P":
            project()
        elif name == "O":
            own_values()
        elif name == "R":
            some_prev(len(waiting))
            ready()
        elif name == "B" and turn * quarter < chunks:
            lax.fori_loop(turn * quarter, turn * quarter + quarter, band_block, 0, unroll=quarter)
            turn += 1
    advance("k")
    advance("v")

    for part in range(2):
        for k in range(half):
            at = (part * half + k) * PAGE
            kpages[at:at + PAGE, :] = flows["k"][part].entry(k)
            vpages_t[:, at:at + PAGE] = flows["v"][part].entry(k).T

    def page_block(i, carry):
        start = pl.multiple_of(i * BLOCK, BLOCK)
        scores = lax.dot_general(kpages[...], queries[i], NT, preferred_element_type=F32)
        page_of = lax.div(code_ref[pl.ds(i, 1), :], listed)
        weights, scales = [], []
        for h in range(PER_KV):
            across = slice(h * BLOCK, (h + 1) * BLOCK)
            piece = scores[:PAGE, across]
            for k in range(1, plisted):
                piece = jnp.where(page_of == k, scores[k * PAGE:(k + 1) * PAGE, across], piece)
            before_top = tops[i, h:h + 1, :]
            top = jnp.maximum(jnp.max(piece, axis=0, keepdims=True), before_top)
            expo = jnp.exp2((piece - top) * FACTOR)
            shrink = jnp.exp2((before_top - top) * FACTOR)
            total = sums_ref[i, h:h + 1, :] * shrink + jnp.sum(expo, axis=0, keepdims=True)
            scales.append((shrink, 1.0 / total))
            weights.append(
                jnp.concatenate([jnp.where(page_of == k, expo, 0.0).astype(BF16) for k in range(plisted)], axis=0)
            )
        mixed = jnp.dot(vpages_t[...], jnp.concatenate(weights, axis=1), preferred_element_type=F32)
        for h in range(PER_KV):
            across = slice(h * BLOCK, (h + 1) * BLOCK)
            shrink, inverse = scales[h]
            value = (mixed_ref[i, :, across] * shrink + mixed[:, across]) * inverse
            out_ref[pl.ds(start, BLOCK), h * HEAD_WIDTH:(h + 1) * HEAD_WIDTH] = value.T.astype(BF16)
        at = pl.ds(start, BLOCK)
        pltpu.make_async_copy(out_ref.at[at], out_hbm.at[at], done.at[i]).start()
        return carry

    lax.fori_loop(0, chunks, page_block, 0, unroll=min(chunks, PAGE_UNROLL))

    for copy in prevs + [idprev, to_pair, back] + to_x:
        copy.wait_send()
    for some in flows.values():
        for flow in some:
            flow.finish()
    for i in range(chunks):
        at = pl.ds(i * BLOCK, BLOCK)
        pltpu.make_async_copy(out_ref.at[at], out_hbm.at[at], done.at[i]).wait()


def fused(ny, nz, ntp, page_list, adapter_list, page_entry, adapter_entry, ids, x, q, k, v, cache, down, up):
    chunks = ids.shape[0]
    tokens = k.shape[0]
    stored, rank, features = down.shape
    listed, plisted = adapter_list.shape[0], page_list.shape[0]
    half = plisted // 2
    vmem = pl.BlockSpec(memory_space=pltpu.VMEM)
    smem = pl.BlockSpec(memory_space=pltpu.SMEM)
    hbm = pl.BlockSpec(memory_space=pltpu.HBM)
    most = max(ny, nz) - 1
    nx = max(ntp // 2 - 1, 1)
    dma = pltpu.SemaphoreType.DMA
    stack = PER_KV * BLOCK
    return pl.pallas_call(
        functools.partial(fused_kernel, ny, nz, ntp),
        out_shape=jax.ShapeDtypeStruct(q.shape, BF16),
        in_specs=[smem, smem, vmem, vmem] + [hbm] * 8,
        out_specs=hbm,
        scratch_shapes=[
            pltpu.VMEM((nz, stored, rank, features), BF16),
            pltpu.VMEM((ny, stored, rank, features), BF16),
            pltpu.VMEM((nz, stored, PAGE, HEAD_WIDTH), BF16),
            pltpu.VMEM((ny, stored, PAGE, HEAD_WIDTH), BF16),
            pltpu.VMEM((max(3 * len(CHAINS[ny]), ny + 1), listed, rank, features), BF16),
            pltpu.VMEM((max(3 * len(CHAINS[nz]), nz + 1), listed, rank, features), BF16),
            pltpu.VMEM((2, ny + 1, half, PAGE, HEAD_WIDTH), BF16),
            pltpu.VMEM((2, nz + 1, half, PAGE, HEAD_WIDTH), BF16),
            pltpu.VMEM(x.shape, BF16),
            pltpu.VMEM(q.shape, BF16),
            pltpu.VMEM(ids.shape, jnp.int32),
            pltpu.VMEM(ids.shape, jnp.int32),
            pltpu.VMEM(ids.shape, jnp.int32),
            pltpu.VMEM((listed * rank, features), BF16),
            pltpu.VMEM((listed * rank, features), BF16),
            pltpu.VMEM((2 * tokens, HEAD_WIDTH), BF16),
            pltpu.VMEM((2 * tokens, HEAD_WIDTH), BF16),
            pltpu.VMEM((HEAD_WIDTH, 2 * tokens), BF16),
            pltpu.VMEM((2 * tokens, BLOCK), jnp.int32),
            pltpu.VMEM((plisted * PAGE, HEAD_WIDTH), BF16),
            pltpu.VMEM((HEAD_WIDTH, plisted * PAGE), BF16),
            pltpu.VMEM((chunks, rank, BLOCK), F32),
            pltpu.VMEM((chunks // 2, rank, BLOCK), F32),
            pltpu.VMEM((chunks // 2, rank, BLOCK), F32),
            pltpu.VMEM((nx, chunks // 2, rank, BLOCK), F32),
            pltpu.VMEM((chunks, rank, BLOCK), BF16),
            pltpu.VMEM((chunks, stack, HEAD_WIDTH), BF16),
            pltpu.VMEM((chunks, 8, BLOCK), F32),
            pltpu.VMEM((chunks, 8, BLOCK), F32),
            pltpu.VMEM((chunks, HEAD_WIDTH, stack), F32),
            pltpu.VMEM(q.shape, BF16),
            dma((4, most)), dma((4, most)), dma((2, 4, 2)), dma((2, 4, 2)), dma((6, most)), dma((6, most)),
            dma((3, PREV_PARTS)), dma((3, PREV_PARTS)),
            dma((2,)), dma((2,)), dma((nx,)), dma((nx,)),
            dma((9,)), dma((chunks,)),
        ],
        compiler_params=pltpu.CompilerParams(
            collective_id=0, has_side_effects=True, vmem_limit_bytes=56 * 1024 * 1024
        ),
        name="fused",
    )(page_list, adapter_list, page_entry, adapter_entry, ids, x, q, k, v, cache, down, up)


def solution(mesh, nz=8):
    groups, ntp = mesh.shape["grp"], mesh.shape["tp"]
    ny = groups // nz

    def local(x, q, k, v, request, cache, down, up, page_list, adapter_list, page_entry, adapter_entry):
        return fused(
            ny, nz, ntp, page_list.T, adapter_list.T, page_entry.reshape(1, -1), adapter_entry.reshape(1, -1),
            request.reshape(-1, BLOCK), x, q, k, v, cache, down, up,
        )

    placed = (
        P("grp", "tp"),
        P("grp", "tp"),
        P("grp", "tp"),
        P("grp", "tp"),
        P("grp"),
        P("grp", None, None, "tp"),
        P("grp", None, "tp"),
        P("grp", None, "tp"),
        P(),
        P(),
        P(),
        P(),
    )
    return jax.shard_map(local, mesh=mesh, in_specs=placed, out_specs=P("grp", "tp"), check_vma=False)
```

```python
import functools
import math

import jax
import jax.numpy as jnp
from jax import lax
from jax.experimental import pallas as pl
from jax.experimental.pallas import tpu as pltpu
from jax.sharding import PartitionSpec as P

PER_KV = 4
HEAD_WIDTH = 128
PAGE = 128
BLOCK = 128
ADAPTER_SCALE = 0.5
MESH = pl.DeviceIdType.MESH
F32 = jnp.float32
BF16 = jnp.bfloat16


def ring_split(n, heavy_right):
    more, fewer = n // 2, (n - 1) // 2
    return (more, fewer) if heavy_right else (fewer, more)


def token_codes(ids_row, table_columns):
    requests = table_columns.shape[0]
    numbers = lax.broadcasted_iota(jnp.int32, (requests, ids_row.shape[1]), 0)
    return jnp.sum(jnp.where(numbers == ids_row, table_columns, 0), axis=0, keepdims=True)


def as_columns(row):
    return jnp.broadcast_to(row, (128, row.shape[1])).T


class Gather:
    def __init__(self, table, pos, n, peers, split, send, recv):
        self.copies = []
        for s in range(1, max(split) + 1):
            now = []
            for way in (0, 1):
                if s <= split[way]:
                    origin = lax.rem(pos - (s - 1) + n, n) if way == 0 else lax.rem(pos + (s - 1), n)
                    at = s - 1 if way == 0 else split[0] + s - 1
                    now.append(remote(table.at[origin], table.at[origin], send.at[at], recv.at[at], peers[way]))
                else:
                    now.append(None)
            self.copies.append(now)
        self.steps = len(self.copies)

    def start(self):
        for copy in self.copies[0]:
            if copy is not None:
                copy.start()

    def forward(self, s):
        for way, copy in enumerate(self.copies[s]):
            if copy is not None:
                copy.wait_recv()
                if s + 1 < self.steps and self.copies[s + 1][way] is not None:
                    self.copies[s + 1][way].start()

    def finish(self):
        for now in self.copies:
            for copy in now:
                if copy is not None:
                    copy.wait_send()


class Slots:
    def __init__(self, load, lists, picks, slots, pos, n, peers, split, send, recv, group_at, index_of, place_of):
        self.load, self.lists, self.picks, self.slots, self.pos, self.n = load, lists, picks, slots, pos, n
        self.split = split
        self.base = (0, split[0] + 1)
        self.group_at, self.index_of, self.place_of = group_at, index_of, place_of
        self.copies = []
        for way in (0, 1):
            base = self.base[way]
            sems = 0 if way == 0 else split[0]
            self.copies.append(
                [
                    remote(slots.at[base + s], slots.at[base + s + 1], send.at[sems + s], recv.at[sems + s], peers[way])
                    for s in range(split[way])
                ]
            )
        self.steps = max(split)
        self.plan = {}

    def prepare(self):
        for way in (0, 1):
            for s in range(self.split[way] + 1):
                away = self.split[way] - s
                target = lax.rem(self.pos + away, self.n) if way == 0 else lax.rem(self.pos - away + self.n, self.n)
                group = self.group_at(target)
                items = [self.lists[k, group] for k in self.picks]
                self.plan[way, s] = [(self.index_of(item), self.place_of(item)) for item in items]

    def fill(self, way, s, wait=None):
        plan = self.plan[way, s]
        mine = [self.load(index) for index, _ in plan]
        if wait is not None:
            wait()
        at = self.base[way] + s
        for k, (_, place) in enumerate(plan):
            value = mine[k]
            if s > 0:
                value = jnp.where(place == self.pos, value, self.slots[at, k])
            self.slots[at, k] = value

    def start(self):
        for way in (0, 1):
            if self.split[way] > 0:
                self.fill(way, 0)
                self.copies[way][0].start()

    def forward(self, s):
        for way in (0, 1):
            if s < self.split[way]:
                copy = self.copies[way][s]
                if s + 1 < self.split[way]:
                    self.fill(way, s + 1, copy.wait_recv)
                    self.copies[way][s + 1].start()
                else:
                    copy.wait_recv()

    def entry(self, k):
        rights, lefts = self.split
        index, place = self.plan[0, rights][k]
        value = self.load(index)
        ahead = lax.rem(place - self.pos + self.n, self.n)
        if rights > 0:
            value = jnp.where(ahead > lefts, self.slots[rights, k], value)
        if lefts > 0:
            value = jnp.where((ahead > 0) & (ahead <= lefts), self.slots[rights + 1 + lefts, k], value)
        return value

    def finish(self):
        for way in (0, 1):
            for copy in self.copies[way]:
                copy.wait_send()


class Spread:
    def __init__(self, table, pos, n, peer_at, send, recv):
        order = sorted(range(1, n), key=lambda d: -min(d, n - d))
        self.copies = [remote(table.at[pos], table.at[pos], send.at[d - 1], recv.at[d - 1], peer_at(d)) for d in order]

    def start(self):
        for copy in self.copies:
            copy.start()

    steps = 1

    def forward(self, s):
        for copy in self.copies:
            copy.wait_recv()

    def finish(self):
        for copy in self.copies:
            copy.wait_send()


CHAINS = {8: ((-4, -3), (-2, -1), (2, 1), (3,)), 4: ((-2, -1), (1,)), 2: ((-1,),)}


class Relay:
    def __init__(self, table, lists, slots, pos, n, peer_at, send, recv, group_at, index_of, place_of, mirror=False):
        self.table, self.slots, self.pos, self.n = table, slots, pos, n
        self.chains = CHAINS[n]
        if mirror and n > 2:
            self.chains = tuple(tuple(-offset for offset in chain) for chain in self.chains)
        self.plan, self.first, self.second = {}, [], []
        count = lists.shape[0]
        targets = [0] + [-offset for chain in self.chains for offset in chain]
        for away in targets:
            group = group_at(lax.rem(pos + away + n, n))
            items = [lists[k, group] for k in range(count)]
            self.plan[away] = [(index_of(item), place_of(item)) for item in items]
        for c, chain in enumerate(self.chains):
            at = 3 * c
            if len(chain) == 1:
                self.first.append(remote(slots.at[at], slots.at[at + 2], send.at[c, 0], recv.at[c, 0], peer_at(-chain[0])))
                self.second.append(None)
            else:
                self.first.append(
                    remote(slots.at[at], slots.at[at + 1], send.at[c, 0], recv.at[c, 0], peer_at(chain[1] - chain[0]))
                )
                self.second.append(
                    remote(slots.at[at + 1], slots.at[at + 2], send.at[c, 1], recv.at[c, 1], peer_at(-chain[1]))
                )

    def start(self):
        for c, chain in enumerate(self.chains):
            for k, (index, _) in enumerate(self.plan[-chain[0]]):
                self.slots[3 * c, k] = self.table[index]
            self.first[c].start()

    steps = 2

    def forward(self, s):
        if s == 1:
            for c, chain in enumerate(self.chains):
                (self.first if len(chain) == 1 else self.second)[c].wait_recv()
            return
        for c, chain in enumerate(self.chains):
            if len(chain) == 2:
                plan = self.plan[-chain[1]]
                mine = [self.table[index] for index, _ in plan]
                self.first[c].wait_recv()
                for k, (_, place) in enumerate(plan):
                    self.slots[3 * c + 1, k] = jnp.where(place == self.pos, mine[k], self.slots[3 * c + 1, k])
                self.second[c].start()

    def entry(self, k):
        index, place = self.plan[0][k]
        value = self.table[index]
        ahead = lax.rem(place - self.pos + self.n, self.n)
        for c, chain in enumerate(self.chains):
            here = ahead == (chain[0] + self.n) % self.n
            if len(chain) == 2:
                here = here | (ahead == (chain[1] + self.n) % self.n)
            value = jnp.where(here, self.slots[3 * c + 2, k], value)
        return value

    def finish(self):
        for copy in self.first + [copy for copy in self.second if copy is not None]:
            copy.wait_send()


def remote(src, dst, send, recv, peer):
    return pltpu.make_async_remote_copy(
        src_ref=src, dst_ref=dst, send_sem=send, recv_sem=recv, device_id=peer, device_id_type=MESH
    )


PREV_PARTS = 4
PAGE_UNROLL = 4
DIRECT = "du"
SCHEDULE = (
    "D0", "U0", "K0", "V0", "p1", "D1", "U1", "K1", "V1", "p1", "D2", "U2",
    "K2", "V2", "p2", "D3", "U3", "d*", "u*", "K3", "V3", "d0", "u0", "p8",
    "k*", "v*", "P", "O", "k0", "v0", "R", "k1", "v1", "B", "B", "k2",
    "v2", "B", "B",
)
FACTOR = math.log2(math.e) * HEAD_WIDTH ** -0.5
NT = (((1,), (1,)), ((), ()))
TN = (((0,), (0,)), ((), ()))


def fused_kernel(
    ny, nz, ntp,
    page_list, adapter_list, page_entry_ref, adapter_entry_ref,
    ids_hbm, x_hbm, q_hbm, k_hbm, v_hbm, cache_hbm, down_hbm, up_hbm,
    out_hbm,
    down_tab, up_tab, kpage_tab, vpage_tab,
    down_slots, up_slots, kpage_slots, vpage_slots,
    x_ref, q_ref, ids_ref, idprev_ref, code_ref, down_all, up_all,
    keys, values, values_t, key_ids, kpages, vpages_t,
    parts, from_pair, half_sum, from_x, lowrank_ref,
    queries, tops, sums_ref, mixed_ref, out_ref,
    gather_send, gather_recv, relay_send, relay_recv, slot_send, slot_recv, prev_send, prev_recv, pair_send, pair_recv, x_send, x_recv,
    here, done,
):
    group = lax.axis_index("grp")
    tp = lax.axis_index("tp")
    groups = ny * nz
    y, z = lax.div(group, nz), lax.rem(group, nz)
    z_peers = ((y * nz + lax.rem(z + 1, nz), tp), (y * nz + lax.rem(z + nz - 1, nz), tp))
    y_peers = ((lax.rem(y + 1, ny) * nz + z, tp), (lax.rem(y + ny - 1, ny) * nz + z, tp))
    after = (lax.rem(group + 1, groups), tp)
    before = (lax.rem(group + groups - 1, groups), tp)
    core = lax.rem(tp, 2)
    pair = (group, tp + 1 - 2 * core)
    x_peers = [(group, lax.rem(tp + 2 * d, ntp)) for d in range(1, ntp // 2)]

    barrier = pltpu.get_barrier_semaphore()
    def z_at(offset):
        return (y * nz + lax.rem(z + offset + nz, nz), tp)

    def y_at(offset):
        return (lax.rem(y + offset + ny, ny) * nz + z, tp)

    greeted = [z_at(d) for d in range(1, nz)] + [y_at(d) for d in range(1, ny)] + [after, before, pair] + x_peers
    for peer in greeted:
        pl.semaphore_signal(barrier, inc=1, device_id=peer, device_id_type=MESH)

    stored, rank = down_hbm.shape[0], down_hbm.shape[1]
    tokens = k_hbm.shape[0]
    chunks = tokens // BLOCK
    listed, plisted = adapter_list.shape[0], page_list.shape[0]
    half = plisted // 2

    own = [
        pltpu.make_async_copy(down_hbm, down_tab.at[z], here.at[0]),
        pltpu.make_async_copy(up_hbm, up_tab.at[y], here.at[1]),
        pltpu.make_async_copy(cache_hbm.at[:, 0], kpage_tab.at[z], here.at[2]),
        pltpu.make_async_copy(cache_hbm.at[:, 1], vpage_tab.at[y], here.at[3]),
    ]
    own_rows = pl.ds(tokens, tokens)
    staged = [
        pltpu.make_async_copy(ids_hbm, ids_ref, here.at[4]),
        pltpu.make_async_copy(x_hbm, x_ref, here.at[5]),
        pltpu.make_async_copy(q_hbm, q_ref, here.at[6]),
        pltpu.make_async_copy(k_hbm, keys.at[own_rows], here.at[7]),
        pltpu.make_async_copy(v_hbm, values.at[own_rows], here.at[8]),
    ]
    for copy in own + staged:
        copy.start()

    zs, ys = ring_split(nz, False), ring_split(ny, True)
    by_y = (lambda target: target * nz + z, lambda item: (lax.rem(lax.div(item, stored), nz), lax.rem(item, stored)),
            lambda item: lax.div(item, stored * nz))
    by_z = (lambda target: y * nz + target, lambda item: (lax.div(item, stored * nz), lax.rem(item, stored)),
            lambda item: lax.rem(lax.div(item, stored), nz))

    def gather_z(direct, table, at):
        if direct:
            return Spread(table, z, nz, z_at, gather_send.at[at], gather_recv.at[at])
        return Gather(table, z, nz, z_peers, zs, gather_send.at[at], gather_recv.at[at])

    def gather_y(direct, table, at):
        if direct:
            return Spread(table, y, ny, y_at, gather_send.at[at], gather_recv.at[at])
        return Gather(table, y, ny, y_peers, ys, gather_send.at[at], gather_recv.at[at])

    def slots_y(relay, table, lists, picks, slots, at):
        if relay:
            return Relay(table, lists, slots, y, ny, y_at, relay_send.at[at], relay_recv.at[at], *by_y)
        ring = Slots(
            lambda index: table[index], lists, picks, slots, y, ny, y_peers, ys, slot_send.at[at], slot_recv.at[at], *by_y
        )
        ring.prepare()
        return ring

    def slots_z(relay, table, lists, picks, slots, at):
        if relay:
            return Relay(table, lists, slots, z, nz, z_at, relay_send.at[at], relay_recv.at[at], *by_z, mirror=True)
        ring = Slots(
            lambda index: table[index], lists, picks, slots, z, nz, z_peers, zs, slot_send.at[at], slot_recv.at[at], *by_z
        )
        ring.prepare()
        return ring

    flows = {
        "D": [gather_z("D" in DIRECT, down_tab, 0)],
        "U": [gather_y("U" in DIRECT, up_tab, 1)],
        "K": [gather_z("K" in DIRECT, kpage_tab, 2)],
        "V": [gather_y("V" in DIRECT, vpage_tab, 3)],
    }
    every = range(listed)

    def make_slots():
        flows["d"] = [slots_y("d" in DIRECT, down_tab, adapter_list, every, down_slots, 0)]
        flows["u"] = [slots_z("u" in DIRECT, up_tab, adapter_list, every, up_slots, 1)]
        flows["k"], flows["v"] = [], []
        for part in range(2):
            picks = range(part * half, part * half + half)
            flows["k"].append(slots_y(False, kpage_tab, page_list, picks, kpage_slots.at[part], 2 + part))
            flows["v"].append(slots_z(False, vpage_tab, page_list, picks, vpage_slots.at[part], 4 + part))

    state = {name: 0 for name in "DUKVduvk"}

    def advance(name, upto=None):
        steps = max(flow.steps for flow in flows[name])
        while state[name] < (steps if upto is None else min(upto, steps)):
            for flow in flows[name]:
                if state[name] < flow.steps:
                    flow.forward(state[name])
            state[name] += 1

    rows = tokens // PREV_PARTS
    prevs = []
    for part in range(PREV_PARTS):
        at = pl.ds(part * rows, rows)
        prevs.append(remote(k_hbm.at[at], keys.at[at], prev_send.at[0, part], prev_recv.at[0, part], after))
        prevs.append(remote(v_hbm.at[at], values.at[at], prev_send.at[1, part], prev_recv.at[1, part], after))
    idprev = remote(ids_hbm, idprev_ref, prev_send.at[2, 0], prev_recv.at[2, 0], after)
    waiting = list(prevs)

    def some_prev(count):
        for _ in range(min(count, len(waiting))):
            waiting.pop(0).start()

    pl.semaphore_wait(barrier, len(greeted))
    for copy, name in zip(own, "DUKV"):
        copy.wait()
        flows[name][0].start()
    idprev.start()
    make_slots()
    staged[0].wait()
    code_columns = as_columns(page_entry_ref[...] * listed + adapter_entry_ref[...])
    for c in range(chunks):
        code_ref[pl.ds(c, 1), :] = token_codes(ids_ref[pl.ds(c, 1), :], code_columns)
        key_ids[pl.ds(tokens + c * BLOCK, BLOCK), :] = as_columns(ids_ref[pl.ds(c, 1), :])

    each = chunks // 2
    mine = pl.ds(core * each, each)
    theirs = pl.ds((1 - core) * each, each)
    to_pair = remote(parts.at[theirs], from_pair, pair_send.at[0], pair_recv.at[0], pair)
    to_x = [
        remote(half_sum, from_x.at[d], x_send.at[d], x_recv.at[d], peer) for d, peer in enumerate(x_peers)
    ]
    back = remote(lowrank_ref.at[mine], lowrank_ref.at[mine], pair_send.at[1], pair_recv.at[1], pair)

    def project():
        advance("d")
        for k in range(listed):
            down_all[k * rank:(k + 1) * rank, :] = flows["d"][0].entry(k)
        staged[1].wait()
        partial = lax.dot_general(down_all[...], x_ref[...], NT, preferred_element_type=F32)
        for c in range(chunks):
            entry = lax.rem(code_ref[pl.ds(c, 1), :], listed)
            total = jnp.zeros((rank, BLOCK), F32)
            for k in range(listed):
                total = jnp.where(entry == k, partial[k * rank:(k + 1) * rank, c * BLOCK:(c + 1) * BLOCK], total)
            parts[c] = total
        to_pair.start()
        to_pair.wait_recv()
        half_sum[...] = parts[mine] + from_pair[...]
        for copy in to_x:
            copy.start()

    def own_values():
        for copy in staged[2:]:
            copy.wait()
        for c in range(chunks):
            at = tokens + c * BLOCK
            values_t[:, at:at + BLOCK] = values[at:at + BLOCK, :].T

    def ready():
        for copy in prevs + [idprev]:
            copy.wait_recv()
        first = group == 0
        for c in range(chunks):
            at = c * BLOCK
            values_t[:, at:at + BLOCK] = values[at:at + BLOCK, :].T
            key_ids[at:at + BLOCK, :] = as_columns(jnp.where(first, -1, idprev_ref[pl.ds(c, 1), :]))
        advance("u")
        for k in range(listed):
            up_all[k * rank:(k + 1) * rank, :] = flows["u"][0].entry(k)
        total = half_sum[...]
        for d, copy in enumerate(to_x):
            copy.wait_recv()
            total = total + from_x[d]
        lowrank_ref[mine] = total.astype(BF16)
        back.start()
        back.wait_recv()

    band = tokens + BLOCK
    later = lax.broadcasted_iota(jnp.int32, (BLOCK, BLOCK), 0)
    sooner = lax.broadcasted_iota(jnp.int32, (BLOCK, BLOCK), 1)
    causal = later <= sooner

    def band_block(i, carry):
        start = pl.multiple_of(i * BLOCK, BLOCK)
        entry = lax.rem(code_ref[pl.ds(i, 1), :], listed)
        low = lowrank_ref[i]
        wide = jnp.concatenate([jnp.where(entry == k, low, jnp.zeros_like(low)) for k in range(listed)], axis=0)
        update = lax.dot_general(wide, up_all[...], TN, preferred_element_type=F32)
        query = (q_ref[pl.ds(start, BLOCK), :].astype(F32) + ADAPTER_SCALE * update).astype(BF16)
        stacked = jnp.concatenate([query[:, h * HEAD_WIDTH:(h + 1) * HEAD_WIDTH] for h in range(PER_KV)], axis=0)
        queries[i] = stacked
        scores = lax.dot_general(keys[pl.ds(start, band), :], stacked, NT, preferred_element_type=F32)
        ids_row = ids_ref[pl.ds(i, 1), :]
        masks = [key_ids[pl.ds(start + c * BLOCK, BLOCK), :] == ids_row for c in range(chunks + 1)]
        masks[chunks] = masks[chunks] & causal
        weights = []
        for h in range(PER_KV):
            across = slice(h * BLOCK, (h + 1) * BLOCK)
            pieces = [
                jnp.where(masks[c], scores[c * BLOCK:(c + 1) * BLOCK, across], F32(-1e30)) for c in range(chunks + 1)
            ]
            top = jnp.max(functools.reduce(jnp.maximum, pieces), axis=0, keepdims=True)
            expos = [jnp.exp2((piece - top) * FACTOR) for piece in pieces]
            tops[i, h:h + 1, :] = top
            sums_ref[i, h:h + 1, :] = jnp.sum(functools.reduce(jnp.add, expos), axis=0, keepdims=True)
            weights.append(jnp.concatenate([e.astype(BF16) for e in expos], axis=0))
        mixed_ref[i] = jnp.dot(
            values_t[:, pl.ds(start, band)], jnp.concatenate(weights, axis=1), preferred_element_type=F32
        )
        return carry

    quarter = max(chunks // 4, 1)
    turn = 0
    for token in SCHEDULE:
        name, what = token[0], token[1:]
        if name in state:
            if what == "*":
                advance(name.upper())
                for flow in flows[name]:
                    flow.start()
            else:
                advance(name, int(what) + 1)
        elif name == "p":
            some_prev(int(what))
        elif name == "P":
            project()
        elif name == "O":
            own_values()
        elif name == "R":
            some_prev(len(waiting))
            ready()
        elif name == "B" and turn * quarter < chunks:
            lax.fori_loop(turn * quarter, turn * quarter + quarter, band_block, 0, unroll=quarter)
            turn += 1
    advance("k")
    advance("v")

    for part in range(2):
        for k in range(half):
            at = (part * half + k) * PAGE
            kpages[at:at + PAGE, :] = flows["k"][part].entry(k)
            vpages_t[:, at:at + PAGE] = flows["v"][part].entry(k).T

    def page_block(i, carry):
        start = pl.multiple_of(i * BLOCK, BLOCK)
        scores = lax.dot_general(kpages[...], queries[i], NT, preferred_element_type=F32)
        page_of = lax.div(code_ref[pl.ds(i, 1), :], listed)
        weights, scales = [], []
        for h in range(PER_KV):
            across = slice(h * BLOCK, (h + 1) * BLOCK)
            piece = scores[:PAGE, across]
            for k in range(1, plisted):
                piece = jnp.where(page_of == k, scores[k * PAGE:(k + 1) * PAGE, across], piece)
            before_top = tops[i, h:h + 1, :]
            top = jnp.maximum(jnp.max(piece, axis=0, keepdims=True), before_top)
            expo = jnp.exp2((piece - top) * FACTOR)
            shrink = jnp.exp2((before_top - top) * FACTOR)
            total = sums_ref[i, h:h + 1, :] * shrink + jnp.sum(expo, axis=0, keepdims=True)
            scales.append((shrink, 1.0 / total))
            weights.append(
                jnp.concatenate([jnp.where(page_of == k, expo, 0.0).astype(BF16) for k in range(plisted)], axis=0)
            )
        mixed = jnp.dot(vpages_t[...], jnp.concatenate(weights, axis=1), preferred_element_type=F32)
        for h in range(PER_KV):
            across = slice(h * BLOCK, (h + 1) * BLOCK)
            shrink, inverse = scales[h]
            value = (mixed_ref[i, :, across] * shrink + mixed[:, across]) * inverse
            out_ref[pl.ds(start, BLOCK), h * HEAD_WIDTH:(h + 1) * HEAD_WIDTH] = value.T.astype(BF16)
        at = pl.ds(start, BLOCK)
        pltpu.make_async_copy(out_ref.at[at], out_hbm.at[at], done.at[i]).start()
        return carry

    lax.fori_loop(0, chunks, page_block, 0, unroll=min(chunks, PAGE_UNROLL))

    for copy in prevs + [idprev, to_pair, back] + to_x:
        copy.wait_send()
    for some in flows.values():
        for flow in some:
            flow.finish()
    for i in range(chunks):
        at = pl.ds(i * BLOCK, BLOCK)
        pltpu.make_async_copy(out_ref.at[at], out_hbm.at[at], done.at[i]).wait()


def fused(ny, nz, ntp, page_list, adapter_list, page_entry, adapter_entry, ids, x, q, k, v, cache, down, up):
    chunks = ids.shape[0]
    tokens = k.shape[0]
    stored, rank, features = down.shape
    listed, plisted = adapter_list.shape[0], page_list.shape[0]
    half = plisted // 2
    vmem = pl.BlockSpec(memory_space=pltpu.VMEM)
    smem = pl.BlockSpec(memory_space=pltpu.SMEM)
    hbm = pl.BlockSpec(memory_space=pltpu.HBM)
    most = max(ny, nz) - 1
    nx = max(ntp // 2 - 1, 1)
    dma = pltpu.SemaphoreType.DMA
    stack = PER_KV * BLOCK
    return pl.pallas_call(
        functools.partial(fused_kernel, ny, nz, ntp),
        out_shape=jax.ShapeDtypeStruct(q.shape, BF16),
        in_specs=[smem, smem, vmem, vmem] + [hbm] * 8,
        out_specs=hbm,
        scratch_shapes=[
            pltpu.VMEM((nz, stored, rank, features), BF16),
            pltpu.VMEM((ny, stored, rank, features), BF16),
            pltpu.VMEM((nz, stored, PAGE, HEAD_WIDTH), BF16),
            pltpu.VMEM((ny, stored, PAGE, HEAD_WIDTH), BF16),
            pltpu.VMEM((max(3 * len(CHAINS[ny]), ny + 1), listed, rank, features), BF16),
            pltpu.VMEM((max(3 * len(CHAINS[nz]), nz + 1), listed, rank, features), BF16),
            pltpu.VMEM((2, ny + 1, half, PAGE, HEAD_WIDTH), BF16),
            pltpu.VMEM((2, nz + 1, half, PAGE, HEAD_WIDTH), BF16),
            pltpu.VMEM(x.shape, BF16),
            pltpu.VMEM(q.shape, BF16),
            pltpu.VMEM(ids.shape, jnp.int32),
            pltpu.VMEM(ids.shape, jnp.int32),
            pltpu.VMEM(ids.shape, jnp.int32),
            pltpu.VMEM((listed * rank, features), BF16),
            pltpu.VMEM((listed * rank, features), BF16),
            pltpu.VMEM((2 * tokens, HEAD_WIDTH), BF16),
            pltpu.VMEM((2 * tokens, HEAD_WIDTH), BF16),
            pltpu.VMEM((HEAD_WIDTH, 2 * tokens), BF16),
            pltpu.VMEM((2 * tokens, BLOCK), jnp.int32),
            pltpu.VMEM((plisted * PAGE, HEAD_WIDTH), BF16),
            pltpu.VMEM((HEAD_WIDTH, plisted * PAGE), BF16),
            pltpu.VMEM((chunks, rank, BLOCK), F32),
            pltpu.VMEM((chunks // 2, rank, BLOCK), F32),
            pltpu.VMEM((chunks // 2, rank, BLOCK), F32),
            pltpu.VMEM((nx, chunks // 2, rank, BLOCK), F32),
            pltpu.VMEM((chunks, rank, BLOCK), BF16),
            pltpu.VMEM((chunks, stack, HEAD_WIDTH), BF16),
            pltpu.VMEM((chunks, 8, BLOCK), F32),
            pltpu.VMEM((chunks, 8, BLOCK), F32),
            pltpu.VMEM((chunks, HEAD_WIDTH, stack), F32),
            pltpu.VMEM(q.shape, BF16),
            dma((4, most)), dma((4, most)), dma((2, 4, 2)), dma((2, 4, 2)), dma((6, most)), dma((6, most)),
            dma((3, PREV_PARTS)), dma((3, PREV_PARTS)),
            dma((2,)), dma((2,)), dma((nx,)), dma((nx,)),
            dma((9,)), dma((chunks,)),
        ],
        compiler_params=pltpu.CompilerParams(
            collective_id=0, has_side_effects=True, vmem_limit_bytes=56 * 1024 * 1024
        ),
        name="fused",
    )(page_list, adapter_list, page_entry, adapter_entry, ids, x, q, k, v, cache, down, up)


def solution(mesh, nz=8):
    groups, ntp = mesh.shape["grp"], mesh.shape["tp"]
    ny = groups // nz

    def local(x, q, k, v, request, cache, down, up, page_list, adapter_list, page_entry, adapter_entry):
        return fused(
            ny, nz, ntp, page_list.T, adapter_list.T, page_entry.reshape(1, -1), adapter_entry.reshape(1, -1),
            request.reshape(-1, BLOCK), x, q, k, v, cache, down, up,
        )

    placed = (
        P("grp", "tp"),
        P("grp", "tp"),
        P("grp", "tp"),
        P("grp", "tp"),
        P("grp"),
        P("grp", None, None, "tp"),
        P("grp", None, "tp"),
        P("grp", None, "tp"),
        P(),
        P(),
        P(),
        P(),
    )
    return jax.shard_map(local, mesh=mesh, in_specs=placed, out_specs=P("grp", "tp"), check_vma=False)
```
